32 devices in a mesh: grid: 8 (over y, x, core), pt: 4 (over z).
Axes of the slice: x: 2, y: 2, z: 4, core: 2. Of those that a mesh axis runs over, the one named last changes fastest.
Arguments:
- orbitals: bfloat16 [2048, 4096], P('grid'), may hold values from -0.875 to 0.875
- point_index: int32 [2048], P('pt'), may hold values from 0 to 4095, as said below
- factor_panels: float32 [2048, 1024], P('pt'), as said below
Outputs:
- solved: float32 [4096, 2048], P('grid', 'pt')
The draws below stay inside these ranges and needn't reach their ends.
Inputs may be any that keep to these rules, and one draw needn't show every extreme that they name: `point_index`: all entries are different; 0 and 4095 are always among them. `factor_panels`: lower triangular in its global row and column indices, diagonal between 1.5 and 3.
All inputs are finite; a program needn't handle non-finite values.
Results may differ from the reference program's by a relative error of at most 0.0018.
Values may be sent and summed in bfloat16 or wider, within the bound.
A program may use at most 64 MiB of HBM per device.

```python
import math
import jax
import jax.numpy as jnp
from jax import lax

NORB = 2048
PANEL = 512
ROWS = 4096
NPTS = 2048


def draw_point_index(key, part):
    first_key, second_key = jax.random.split(jax.random.fold_in(key, 11))
    inner = jax.random.permutation(first_key, ROWS - 2)[:NPTS - 2].astype(jnp.int32) + 1
    ends = jnp.array([0, ROWS - 1], jnp.int32)
    chosen = jnp.concatenate([ends, inner])
    return jax.random.permutation(second_key, chosen).astype(jnp.int32)


def draw_factor_panels(key, part):
    first_key, second_key = jax.random.split(jax.random.fold_in(key, 23))
    row_ids = jnp.arange(NPTS)[:, None]
    col_ids = jnp.arange(2 * PANEL)[None, :]
    sigma = 0.6 / jnp.sqrt(2.0 * PANEL)
    off_diag = jax.random.normal(first_key, (NPTS, 2 * PANEL), jnp.float32) * sigma
    diag_vals = jnp.exp(jax.random.uniform(second_key, (NPTS, 1), jnp.float32, jnp.log(1.5), jnp.log(3.0)))
    lowered = jnp.where(col_ids < row_ids, off_diag, jnp.where(col_ids == row_ids, diag_vals, 0.0))
    return lowered.astype(jnp.float32)


def level_of(rng, extent, shards, smallest, top_value):
    gain, own = 1.0, jax.random.fold_in(rng, 6)
    for axis_at, parts in shards:
        draws = jnp.exp(jax.random.uniform(jax.random.fold_in(own, axis_at), (parts,), jnp.float32, smallest / len(shards), top_value / len(shards)))
        gain = gain * jnp.repeat(draws, extent[axis_at] // parts).reshape([-1 if axis == axis_at else 1 for axis in range(len(extent))])
    return gain


def scatter_about(stream_key, extent, spread, reach, cuts=(), dtype=jnp.bfloat16):
    values = jax.random.normal(stream_key, extent, jnp.float32) * spread
    if len(cuts) > 0:
        values = level_of(stream_key, extent, cuts, -0.22, 0.18) * values
    return jnp.clip(values, min=-reach, max=reach).astype(dtype)


def setup_inputs(seed: int = 0) -> dict:
    keys = jax.random.split(jax.random.key(seed), 4)
    return {
        "orbitals": scatter_about(keys[0], (NORB, ROWS), (NORB ** -0.25), 0.875, ((0, 8),)),
        "point_index": draw_point_index(jax.random.fold_in(keys[3], 71), 0),
        "factor_panels": draw_factor_panels(jax.random.fold_in(keys[3], 71), 0),
    }


def solve_panel(factor, targets):
    return lax.linalg.triangular_solve(factor, targets, left_side=False, lower=True, transpose_a=True)

def rounded(values):
    return lax.optimization_barrier(values.astype(jnp.bfloat16)).astype(jnp.float32)

def reference(orbitals, point_index, factor_panels):
    panel_cols = PANEL
    point_orbs = jnp.take(orbitals, point_index.astype(jnp.int32), axis=1).astype(jnp.float32)
    row_step = math.gcd(ROWS, 4096)
    grouped = orbitals.reshape(NORB, ROWS // row_step, row_step).transpose(1, 0, 2)
    diag_first = factor_panels[0:panel_cols, 0:panel_cols]
    diag_second = factor_panels[panel_cols:2 * panel_cols, panel_cols:2 * panel_cols]
    below_first = factor_panels[panel_cols:, 0:panel_cols]
    below_second = factor_panels[2 * panel_cols:, panel_cols:2 * panel_cols]

    def one_block(row_block):
        inner_sums = lax.dot_general(row_block.astype(jnp.float32), point_orbs.astype(jnp.float32), (((0,), (0,)), ((), ())), precision=lax.Precision.HIGHEST, preferred_element_type=jnp.float32)
        products = inner_sums * inner_sums
        first = solve_panel(diag_first, products[:, 0:panel_cols])
        left = products[:, panel_cols:] - jnp.dot(rounded(first), below_first.T, precision=lax.Precision.HIGHEST)
        second = solve_panel(diag_second, left[:, 0:panel_cols])
        trailing = left[:, panel_cols:] - jnp.dot(rounded(second), below_second.T, precision=lax.Precision.HIGHEST)
        return jnp.concatenate([first, second, trailing], axis=1)
    solved = lax.map(one_block, grouped)
    return solved.reshape(ROWS, NPTS)
```

```python
import contextlib
import functools
import jax
import jax.numpy as jnp
from jax import lax
from jax.experimental import pallas as pl
from jax.experimental.pallas import tpu as pltpu
from jax.sharding import PartitionSpec as P

MESH = pl.DeviceIdType.MESH
F32, BF16, I16, I32 = jnp.float32, jnp.bfloat16, jnp.int16, jnp.int32
LANES = 128
PIECE = 32
TOP = 32000.0


def scope(_):
    return contextlib.nullcontext()


def split(value):
    high = value.astype(BF16)
    return high, (value - high.astype(F32)).astype(BF16)


def dot(a, b):
    return jnp.dot(a, b, preferred_element_type=F32)


def exact_dot(a, b):
    return jnp.dot(a, b, preferred_element_type=F32, precision=lax.Precision.HIGHEST)


def over_bands(a, b):
    return lax.dot_general(a, b, (((0,), (0,)), ((), ())), preferred_element_type=F32)


def each(low, high, body):
    if high - low <= 4:
        for i in range(low, high):
            body(i)
    else:
        pl.loop(low, high)(body)


def invert_lower(low, inv):
    size = low.shape[0]
    blocks = size // LANES
    row = lax.broadcasted_iota(jnp.int32, (LANES, LANES), 0)
    col = lax.broadcasted_iota(jnp.int32, (LANES, LANES), 1)
    tiles, parts = [], []
    for i in range(blocks):
        at = slice(i * LANES, (i + 1) * LANES)
        tile = low[at, at]
        tiles.append(tile)
        parts.append(jnp.where(row == col, 1.0 / jnp.where(row == col, tile, 1.0), 0.0))
    half = 1
    level = 0
    while half < LANES:
        rb, cb = row >> level, col >> level
        mask = ((rb >> 1) == (cb >> 1)) & (rb > cb)
        mids = [exact_dot(jnp.where(mask, tiles[i], 0.0), parts[i]) for i in range(blocks)]
        parts = [parts[i] - exact_dot(parts[i], mids[i]) for i in range(blocks)]
        half *= 2
        level += 1
    inv[...] = jnp.zeros_like(inv)
    for i in range(blocks):
        at = slice(i * LANES, (i + 1) * LANES)
        inv[at, at] = parts[i]
    width = LANES
    while width < size:
        for start in range(0, size, 2 * width):
            top = slice(start, start + width)
            bottom = slice(start + width, start + 2 * width)
            mid = exact_dot(low[bottom, top], inv[top, top])
            inv[bottom, top] = -exact_dot(inv[bottom, bottom], mid)
        width *= 2


def kernel(
    grid_count, pt_count, index, orb, fac, out,
    index_v, orb_v, fac_v, near, points, gathered, norms, scales, sent, came,
    low, inv, a_high, a_low, b_high, b_low, firsts, seconds,
    load_sem, index_sem, fac_sem, near_send, near_recv, point_send, point_recv, norm_send, norm_recv,
    part_send, part_recv, first_send, first_recv, second_send, second_recv,
):
    me = lax.axis_index("grid")
    rank = lax.axis_index("pt")
    own_bands, grid_rows = orb.shape
    chunks = near.shape[0]
    panel = index.shape[1]
    piece = firsts.shape[1]
    pieces = LANES // piece
    rows_here = chunks * LANES
    core = lax.rem(me, 2)
    chip = lax.div(me, 2)
    partner = me + 1 - 2 * core
    pairs = grid_count // 2
    last = pt_count - 1
    depth = min(1024, grid_rows)
    steps = grid_rows // depth

    def load(s):
        at = pl.ds(pl.multiple_of(s * depth, depth), depth)
        return pltpu.make_async_copy(orb.at[:, at], orb_v.at[:, at], load_sem.at[s])

    load_index = pltpu.make_async_copy(index, index_v, index_sem)
    load_fac = pltpu.make_async_copy(fac, fac_v, fac_sem)
    load_index.start()
    each(0, steps, lambda s: load(s).start())
    load_fac.start()

    barrier = pltpu.get_barrier_semaphore()

    @pl.loop(1, grid_count)
    def _(k):
        other = lax.rem(me + k, grid_count)
        pl.semaphore_signal(barrier, inc=1, device_id=(other, rank), device_id_type=MESH)

    @pl.when(rank > 0)
    def _():
        pl.semaphore_signal(barrier, inc=1, device_id=(me, rank - 1), device_id_type=MESH)

    @pl.when(rank < last)
    def _():
        pl.semaphore_signal(barrier, inc=1, device_id=(me, rank + 1), device_id_type=MESH)

    with scope("t_load"):
        load_index.wait()
        load(0).wait()

    with scope("t_gather"):
        gathered[...] = jnp.zeros_like(gathered)
        norms[me] = jnp.zeros(norms.shape[1:], F32)

        @pl.loop(0, steps)
        def _(s):
            @pl.when(s > 0)
            def _():
                load(s).wait()

            part = orb_v[:, pl.ds(pl.multiple_of(s * depth, depth), depth)]
            ids = lax.broadcasted_iota(jnp.int32, (depth, panel), 0) + s * depth
            hot = jnp.where(ids == index_v[...], 1.0, 0.0).astype(BF16)
            gathered[...] += dot(part, hot)
            wide = part.astype(F32)
            size = jnp.max(jnp.sum(wide * wide, axis=0, keepdims=True), axis=1, keepdims=True)
            norms[me] = jnp.maximum(norms[me], size)

        points[core] = gathered[...].astype(BF16)

    at_end = (rank == 0) | (rank == last)

    with scope("t_barrier"):
        @pl.when(at_end)
        def _():
            pl.semaphore_wait(barrier, grid_count)

        @pl.when(jnp.logical_not(at_end))
        def _():
            pl.semaphore_wait(barrier, grid_count + 1)

    def norm_copy(g, target):
        return pltpu.make_async_remote_copy(
            src_ref=norms.at[g],
            dst_ref=norms.at[g],
            send_sem=norm_send.at[target],
            recv_sem=norm_recv.at[g],
            device_id=(target, rank),
            device_id_type=MESH,
        )

    def point_copy(slot):
        return pltpu.make_async_remote_copy(
            src_ref=points.at[slot],
            dst_ref=points.at[slot],
            send_sem=point_send,
            recv_sem=point_recv,
            device_id=(partner, rank),
            device_id_type=MESH,
        )

    def near_copy(q, c):
        start = (2 * c + 1 - core) * rows_here + q * LANES
        return pltpu.make_async_remote_copy(
            src_ref=orb_v.at[:, pl.ds(pl.multiple_of(start, LANES), LANES)],
            dst_ref=near.at[q, :, pl.ds(pl.multiple_of(c * LANES, LANES), LANES)],
            send_sem=near_send.at[q],
            recv_sem=near_recv.at[q],
            device_id=(partner, rank),
            device_id_type=MESH,
        )

    norm_copy(me, partner).start()
    point_copy(core).start()
    for q in range(chunks):
        each(0, pairs, lambda c: near_copy(q, c).start())

    @pl.loop(1, grid_count)
    def _(k):
        other = lax.rem(me + k, grid_count)

        @pl.when(other != partner)
        def _():
            norm_copy(me, other).start()

    with scope("t_invert"):
        load_fac.wait()

        @pl.when(rank < 2)
        def _():
            start = pl.multiple_of(rank * panel, panel)
            low[...] = fac_v[:, pl.ds(start, panel)]
            invert_lower(low, inv)

        @pl.when(rank > 0)
        def _():
            a_high[...], a_low[...] = split(fac_v[:, 0:panel].T)

        @pl.when(rank == 0)
        def _():
            a_high[...], a_low[...] = split(inv[...].T)

        @pl.when(rank > 1)
        def _():
            b_high[...], b_low[...] = split(fac_v[:, panel : 2 * panel].T)

        @pl.when(rank == 1)
        def _():
            b_high[...], b_low[...] = split(inv[...].T)

    def bound(c):
        both = norms[2 * c, 0:1, 0:1] + norms[2 * c + 1, 0:1, 0:1]
        return jnp.broadcast_to(jnp.maximum(both, 1e-30), scales.shape[1:])

    with scope("t_partner"):
        norm_copy(partner, me).wait_recv()
        scales[0] = TOP / bound(chip)
        point_copy(1 - core).wait_recv()

    def part_copy(p, i):
        return pltpu.make_async_remote_copy(
            src_ref=sent.at[p, i - 1],
            dst_ref=came.at[p, i - 1],
            send_sem=part_send.at[p],
            recv_sem=part_recv.at[p],
            device_id=(2 * lax.rem(chip + i, pairs) + core, rank),
            device_id_type=MESH,
        )

    def sums(q, c):
        start = (2 * c + core) * rows_here + q * LANES
        mine = orb_v[:, pl.ds(pl.multiple_of(start, LANES), LANES)]
        other = near[q, :, pl.ds(pl.multiple_of(c * LANES, LANES), LANES)]
        return over_bands(mine, points[core]) + over_bands(other, points[1 - core])

    for q in range(chunks):
        with scope("t_near"):
            part = near.at[q]
            pltpu.make_async_copy(part, part, near_recv.at[q]).wait()
        with scope("t_parts"):

            def for_other(i):
                value = sums(q, lax.rem(chip + i, pairs)) * scales[0, 0:1, :]
                coded = jnp.round(value).astype(I32).astype(I16)
                for j in range(pieces):
                    sent[q * pieces + j, i - 1] = coded[j * piece : (j + 1) * piece]

            each(1, pairs, for_other)
            for j in range(pieces):
                each(1, pairs, lambda i: part_copy(q * pieces + j, i).start())
            out[q * LANES : (q + 1) * LANES, :] = sums(q, chip)

    with scope("t_norms"):
        @pl.loop(1, grid_count)
        def _(k):
            other = lax.rem(me + k, grid_count)

            @pl.when(other != partner)
            def _():
                norm_copy(other, me).wait_recv()

        def source_scale(i):
            scales[i] = bound(lax.rem(chip + pairs - i, pairs)) * (1.0 / TOP)

        each(1, pairs, source_scale)

    def chain(buf, p, send_sem, recv_sem):
        return pltpu.make_async_remote_copy(
            src_ref=buf.at[p],
            dst_ref=buf.at[p],
            send_sem=send_sem.at[p],
            recv_sem=recv_sem.at[p],
            device_id=(me, rank + 1),
            device_id_type=MESH,
        )

    def solve(value, high, low_part):
        value_high, value_low = split(value)
        return dot(value_high, high[...]) + (dot(value_high, low_part[...]) + dot(value_low, high[...]))

    def apply(value, high, low_part):
        return dot(value, high[...]) + dot(value, low_part[...])

    @pl.loop(0, chunks * pieces)
    def _(p):
        here = pl.ds(pl.multiple_of(p * piece, piece), piece)
        with scope("t_came"):
            part = came.at[p]
            pltpu.make_async_copy(part, part, part_recv.at[p]).wait()
        with scope("t_sum"):

            def add(i):
                out[here, :] += came[p, i - 1].astype(I32).astype(F32) * scales[i, 0:1, :]

            each(1, pairs, add)
            out[here, :] = out[here, :] * out[here, :]

        with scope("t_first"):
            @pl.when(rank == 0)
            def _():
                first = solve(out[here, :], a_high, a_low)
                out[here, :] = first
                firsts[p] = first.astype(BF16)

            @pl.when(rank > 0)
            def _():
                chain(firsts, p, first_send, first_recv).wait_recv()

            @pl.when(rank < last)
            def _():
                chain(firsts, p, first_send, first_recv).start()

        with scope("t_second"):
            @pl.when(rank > 0)
            def _():
                out[here, :] -= apply(firsts[p], a_high, a_low)

            @pl.when(rank == 1)
            def _():
                second = solve(out[here, :], b_high, b_low)
                out[here, :] = second
                seconds[p] = second.astype(BF16)

            @pl.when(rank > 1)
            def _():
                chain(seconds, p, second_send, second_recv).wait_recv()

            @pl.when((rank > 0) & (rank < last))
            def _():
                chain(seconds, p, second_send, second_recv).start()

        with scope("t_last"):
            @pl.when(rank > 1)
            def _():
                out[here, :] -= apply(seconds[p], b_high, b_low)

    with scope("t_drain"):
        for q in range(chunks):
            part = near.at[q]
            pltpu.make_async_copy(part, part, near_send.at[q]).wait()
        point_copy(core).wait_send()

        @pl.loop(1, grid_count)
        def _(k):
            norm_copy(me, lax.rem(me + k, grid_count)).wait_send()

        @pl.loop(0, chunks * pieces)
        def _(p):
            part = sent.at[p]
            pltpu.make_async_copy(part, part, part_send.at[p]).wait()

            @pl.when(rank < last)
            def _():
                chain(firsts, p, first_send, first_recv).wait_send()

            @pl.when((rank > 0) & (rank < last))
            def _():
                chain(seconds, p, second_send, second_recv).wait_send()


def on_device(grid_count, pt_count, orbitals, point_index, factor_panels):
    own_bands, grid_rows = orbitals.shape
    rows_here = grid_rows // grid_count
    panel = point_index.shape[0]
    chunks = rows_here // LANES
    pairs = grid_count // 2
    pieces = rows_here // PIECE
    hbm = pl.BlockSpec(memory_space=pl.ANY)
    dma = pltpu.SemaphoreType.DMA
    square = [pltpu.VMEM((panel, panel), t) for t in (F32, F32, BF16, BF16, BF16, BF16)]
    scratch = [
        pltpu.VMEM((1, panel), I32),
        pltpu.VMEM((own_bands, grid_rows), BF16),
        pltpu.VMEM(factor_panels.shape, F32),
        pltpu.VMEM((chunks, own_bands, pairs * LANES), BF16),
        pltpu.VMEM((2, own_bands, panel), BF16),
        pltpu.VMEM((own_bands, panel), F32),
        pltpu.VMEM((grid_count, 8, LANES), F32),
        pltpu.VMEM((pairs, 8, panel), F32),
        pltpu.VMEM((pieces, pairs - 1, PIECE, panel), I16),
        pltpu.VMEM((pieces, pairs - 1, PIECE, panel), I16),
        *square,
        pltpu.VMEM((pieces, PIECE, panel), BF16),
        pltpu.VMEM((pieces, PIECE, panel), BF16),
    ]
    used = sum(s.dtype.itemsize * functools.reduce(lambda a, b: a * b, s.shape) for s in scratch)
    sems = [
        dma((grid_rows // min(1024, grid_rows),)),
        dma, dma,
        dma((chunks,)), dma((chunks,)),
        dma, dma,
        dma((grid_count,)), dma((grid_count,)),
        *[dma((pieces,))] * 6,
    ]
    args = [point_index.reshape(1, panel), orbitals, factor_panels]
    return pl.pallas_call(
        functools.partial(kernel, grid_count, pt_count),
        out_shape=jax.ShapeDtypeStruct((rows_here, panel), F32),
        in_specs=[hbm] * 3,
        out_specs=pl.BlockSpec(memory_space=pltpu.VMEM),
        scratch_shapes=scratch + sems,
        compiler_params=pltpu.CompilerParams(
            collective_id=0, has_side_effects=True, vmem_limit_bytes=used + 8 * 1024 * 1024
        ),
    )(*[pltpu.with_memory_space_constraint(a, pltpu.HBM) for a in args])


def solution(mesh):
    in_specs = (P("grid", None), P("pt"), P("pt", None))
    out_specs = P("grid", "pt")
    body = functools.partial(on_device, mesh.shape["grid"], mesh.shape["pt"])
    return jax.shard_map(
        body, mesh=mesh, in_specs=in_specs, out_specs=out_specs, check_vma=False
    )
```

```python
import contextlib
import functools
import jax
import jax.numpy as jnp
from jax import lax
from jax.experimental import pallas as pl
from jax.experimental.pallas import tpu as pltpu
from jax.sharding import PartitionSpec as P

MESH = pl.DeviceIdType.MESH
F32, BF16, I16, I32 = jnp.float32, jnp.bfloat16, jnp.int16, jnp.int32
LANES = 128
PIECE = 32
TOP = 32000.0


def scope(_):
    return contextlib.nullcontext()


def split(value):
    high = value.astype(BF16)
    return high, (value - high.astype(F32)).astype(BF16)


def dot(a, b):
    return jnp.dot(a, b, preferred_element_type=F32)


def fine_dot(a, b):
    size = b.shape[1]
    a_high, a_low = split(a)
    b_high, b_low = split(b)
    if size > LANES:
        return dot(a_high, b_high) + (dot(a_high, b_low) + dot(a_low, b_high))
    left = jnp.concatenate([a_high, a_low], axis=1)
    top = jnp.concatenate([b_high, b_low], axis=1)
    bottom = jnp.concatenate([b_high, jnp.zeros_like(b_high)], axis=1)
    both = dot(left, jnp.concatenate([top, bottom], axis=0))
    return both[:, :size] + both[:, size:]


def over_bands(a, b):
    return lax.dot_general(a, b, (((0,), (0,)), ((), ())), preferred_element_type=F32)


def each(low, high, body):
    if high - low <= 4:
        for i in range(low, high):
            body(i)
    else:
        pl.loop(low, high)(body)


def invert_lower(low, inv):
    size = low.shape[0]
    blocks = size // LANES
    row = lax.broadcasted_iota(jnp.int32, (LANES, LANES), 0)
    col = lax.broadcasted_iota(jnp.int32, (LANES, LANES), 1)
    tiles, parts = [], []
    for i in range(blocks):
        at = slice(i * LANES, (i + 1) * LANES)
        tile = low[at, at]
        tiles.append(tile)
        part = jnp.where(row == col, 1.0 / jnp.where(row == col, tile, 1.0), 0.0)
        below = jnp.where((row >> 1 == col >> 1) & (row > col), tile, 0.0)
        down, across = jnp.sum(part, axis=1, keepdims=True), jnp.sum(part, axis=0, keepdims=True)
        parts.append(part - below * down * across)
    half = 2
    level = 1
    while half < LANES:
        rb, cb = row >> level, col >> level
        mask = ((rb >> 1) == (cb >> 1)) & (rb > cb)
        mids = [fine_dot(jnp.where(mask, tiles[i], 0.0), parts[i]) for i in range(blocks)]
        parts = [parts[i] - fine_dot(parts[i], mids[i]) for i in range(blocks)]
        half *= 2
        level += 1
    inv[...] = jnp.zeros_like(inv)
    for i in range(blocks):
        at = slice(i * LANES, (i + 1) * LANES)
        inv[at, at] = parts[i]
    width = LANES
    while width < size:
        for start in range(0, size, 2 * width):
            top = slice(start, start + width)
            bottom = slice(start + width, start + 2 * width)
            mid = fine_dot(low[bottom, top], inv[top, top])
            inv[bottom, top] = -fine_dot(inv[bottom, bottom], mid)
        width *= 2


def kernel(
    grid_count, pt_count, index, orb, fac, out,
    index_v, orb_v, fac_v, near, points, gathered, norms, scales, sent, came,
    low, inv, a_high, a_low, b_high, b_low, firsts, seconds,
    load_sem, index_sem, fac_sem, near_send, near_recv, point_send, point_recv, norm_send, norm_recv,
    part_send, part_recv, first_send, first_recv, second_send, second_recv,
):
    me = lax.axis_index("grid")
    rank = lax.axis_index("pt")
    own_bands, grid_rows = orb.shape
    chunks = near.shape[0]
    panel = index.shape[1]
    piece = firsts.shape[1]
    pieces = LANES // piece
    rows_here = chunks * LANES
    core = lax.rem(me, 2)
    chip = lax.div(me, 2)
    partner = me + 1 - 2 * core
    pairs = grid_count // 2
    last = pt_count - 1
    depth = min(1024, grid_rows)
    steps = grid_rows // depth

    def load(s):
        at = pl.ds(pl.multiple_of(s * depth, depth), depth)
        return pltpu.make_async_copy(orb.at[:, at], orb_v.at[:, at], load_sem.at[s])

    load_index = pltpu.make_async_copy(index, index_v, index_sem)
    load_fac = pltpu.make_async_copy(fac, fac_v, fac_sem)
    load_index.start()
    each(0, steps, lambda s: load(s).start())
    load_fac.start()

    barrier = pltpu.get_barrier_semaphore()

    @pl.loop(1, grid_count)
    def _(k):
        other = lax.rem(me + k, grid_count)
        pl.semaphore_signal(barrier, inc=1, device_id=(other, rank), device_id_type=MESH)

    @pl.when(rank > 0)
    def _():
        pl.semaphore_signal(barrier, inc=1, device_id=(me, rank - 1), device_id_type=MESH)

    @pl.when(rank < last)
    def _():
        pl.semaphore_signal(barrier, inc=1, device_id=(me, rank + 1), device_id_type=MESH)

    with scope("t_load"):
        load_index.wait()
        load(0).wait()

    with scope("t_gather"):
        gathered[...] = jnp.zeros_like(gathered)
        norms[me] = jnp.zeros(norms.shape[1:], F32)

        @pl.loop(0, steps)
        def _(s):
            @pl.when(s > 0)
            def _():
                load(s).wait()

            part = orb_v[:, pl.ds(pl.multiple_of(s * depth, depth), depth)]
            ids = lax.broadcasted_iota(jnp.int32, (depth, panel), 0) + s * depth
            hot = jnp.where(ids == index_v[...], 1.0, 0.0).astype(BF16)
            gathered[...] += dot(part, hot)
            wide = part.astype(F32)
            size = jnp.max(jnp.sum(wide * wide, axis=0, keepdims=True), axis=1, keepdims=True)
            norms[me] = jnp.maximum(norms[me], size)

        points[core] = gathered[...].astype(BF16)

    at_end = (rank == 0) | (rank == last)

    with scope("t_barrier"):
        @pl.when(at_end)
        def _():
            pl.semaphore_wait(barrier, grid_count)

        @pl.when(jnp.logical_not(at_end))
        def _():
            pl.semaphore_wait(barrier, grid_count + 1)

    def norm_copy(g, target):
        return pltpu.make_async_remote_copy(
            src_ref=norms.at[g],
            dst_ref=norms.at[g],
            send_sem=norm_send,
            recv_sem=norm_recv.at[g],
            device_id=(target, rank),
            device_id_type=MESH,
        )

    def point_copy(slot):
        return pltpu.make_async_remote_copy(
            src_ref=points.at[slot],
            dst_ref=points.at[slot],
            send_sem=point_send,
            recv_sem=point_recv,
            device_id=(partner, rank),
            device_id_type=MESH,
        )

    def near_copy(q, c):
        start = (2 * c + 1 - core) * rows_here + q * LANES
        return pltpu.make_async_remote_copy(
            src_ref=orb_v.at[:, pl.ds(pl.multiple_of(start, LANES), LANES)],
            dst_ref=near.at[q, :, pl.ds(pl.multiple_of(c * LANES, LANES), LANES)],
            send_sem=near_send,
            recv_sem=near_recv.at[q],
            device_id=(partner, rank),
            device_id_type=MESH,
        )

    norm_copy(me, partner).start()
    point_copy(core).start()
    for q in range(chunks):
        each(0, pairs, lambda c: near_copy(q, c).start())

    @pl.loop(1, grid_count)
    def _(k):
        other = lax.rem(me + k, grid_count)

        @pl.when(other != partner)
        def _():
            norm_copy(me, other).start()

    def bound(c):
        both = norms[2 * c, 0:1, 0:1] + norms[2 * c + 1, 0:1, 0:1]
        return jnp.broadcast_to(jnp.maximum(both, 1e-30), scales.shape[1:])

    with scope("t_partner"):
        norm_copy(partner, me).wait_recv()
        scales[0] = TOP / bound(chip)
        point_copy(1 - core).wait_recv()

    def part_copy(p, i):
        return pltpu.make_async_remote_copy(
            src_ref=sent.at[p, i - 1],
            dst_ref=came.at[p, i - 1],
            send_sem=part_send,
            recv_sem=part_recv.at[p],
            device_id=(2 * lax.rem(chip + i, pairs) + core, rank),
            device_id_type=MESH,
        )

    def rows_of(q):
        return pl.ds(pl.multiple_of(q * LANES, LANES), LANES)

    def sums(q, c):
        start = (2 * c + core) * rows_here + q * LANES
        mine = orb_v[:, pl.ds(pl.multiple_of(start, LANES), LANES)]
        other = near[q, :, pl.ds(pl.multiple_of(c * LANES, LANES), LANES)]
        return over_bands(mine, points[core]) + over_bands(other, points[1 - core])

    def send_parts(q):
        with scope("t_near"):
            part = near.at[q]
            pltpu.make_async_copy(part, part, near_recv.at[q]).wait()
        with scope("t_parts"):

            def for_other(i):
                value = sums(q, lax.rem(chip + i, pairs)) * scales[0, 0:1, :]
                coded = jnp.round(value).astype(I32).astype(I16)
                for j in range(pieces):
                    sent[q * pieces + j, i - 1] = coded[j * piece : (j + 1) * piece]

            each(1, pairs, for_other)
            for j in range(pieces):
                each(1, pairs, lambda i: part_copy(q * pieces + j, i).start())
            out[rows_of(q), :] = sums(q, chip)

    send_parts(0)

    with scope("t_invert"):
        load_fac.wait()

        @pl.when(rank < 2)
        def _():
            start = pl.multiple_of(rank * panel, panel)
            low[...] = fac_v[:, pl.ds(start, panel)]
            invert_lower(low, inv)

        @pl.when(rank > 0)
        def _():
            a_high[...], a_low[...] = split(fac_v[:, 0:panel].T)

        @pl.when(rank == 0)
        def _():
            a_high[...], a_low[...] = split(inv[...].T)

        @pl.when(rank > 1)
        def _():
            b_high[...], b_low[...] = split(fac_v[:, panel : 2 * panel].T)

        @pl.when(rank == 1)
        def _():
            b_high[...], b_low[...] = split(inv[...].T)

    with scope("t_norms"):
        @pl.loop(1, grid_count)
        def _(k):
            other = lax.rem(me + k, grid_count)

            @pl.when(other != partner)
            def _():
                norm_copy(other, me).wait_recv()

        def source_scale(i):
            scales[i] = bound(lax.rem(chip + pairs - i, pairs)) * (1.0 / TOP)

        each(1, pairs, source_scale)

    if chunks > 1:
        send_parts(1)

    def chain(buf, p, send_sem, recv_sem):
        return pltpu.make_async_remote_copy(
            src_ref=buf.at[p],
            dst_ref=buf.at[p],
            send_sem=send_sem,
            recv_sem=recv_sem.at[p],
            device_id=(me, rank + 1),
            device_id_type=MESH,
        )

    half = panel // 2

    def solve(value, high, low_part):
        value_high, value_low = split(value)
        both = jnp.concatenate([value_high, value_low], axis=0)

        def columns(k, at):
            wide = dot(both[:, k], high[k, at])
            return wide[:piece] + (dot(value_high[:, k], low_part[k, at]) + wide[piece:])

        left = columns(slice(0, half), slice(0, half))
        right = columns(slice(0, panel), slice(half, panel))
        return jnp.concatenate([left, right], axis=1)

    def apply(value, high, low_part):
        return dot(value, high[...]) + dot(value, low_part[...])

    @pl.loop(0, chunks * pieces)
    def _(p):
        here = pl.ds(pl.multiple_of(p * piece, piece), piece)
        with scope("t_came"):
            part = came.at[p]
            pltpu.make_async_copy(part, part, part_recv.at[p]).wait()
        with scope("t_sum"):

            def add(i):
                out[here, :] += came[p, i - 1].astype(I32).astype(F32) * scales[i, 0:1, :]

            each(1, pairs, add)
            out[here, :] = out[here, :] * out[here, :]

        with scope("t_first"):
            @pl.when(rank == 0)
            def _():
                first = solve(out[here, :], a_high, a_low)
                out[here, :] = first
                firsts[p] = first.astype(BF16)

            @pl.when(rank > 0)
            def _():
                chain(firsts, p, first_send, first_recv).wait_recv()

            @pl.when(rank < last)
            def _():
                chain(firsts, p, first_send, first_recv).start()

        with scope("t_second"):
            @pl.when(rank > 0)
            def _():
                out[here, :] -= apply(firsts[p], a_high, a_low)

            @pl.when(rank == 1)
            def _():
                second = solve(out[here, :], b_high, b_low)
                out[here, :] = second
                seconds[p] = second.astype(BF16)

            @pl.when(rank > 1)
            def _():
                chain(seconds, p, second_send, second_recv).wait_recv()

            @pl.when((rank > 0) & (rank < last))
            def _():
                chain(seconds, p, second_send, second_recv).start()

        with scope("t_last"):
            @pl.when(rank > 1)
            def _():
                out[here, :] -= apply(seconds[p], b_high, b_low)

        @pl.when((lax.rem(p, pieces) == 1) & (p < (chunks - 2) * pieces))
        def _():
            send_parts(lax.div(p, pieces) + 2)

    def sent_all(part, sem):
        pltpu.make_async_copy(part, part, sem).wait()

    with scope("t_drain"):
        sent_all(near, near_send)
        sent_all(sent, part_send)
        sent_all(norms.at[pl.ds(0, grid_count - 1)], norm_send)
        point_copy(core).wait_send()

        @pl.when(rank < last)
        def _():
            sent_all(firsts, first_send)

        @pl.when((rank > 0) & (rank < last))
        def _():
            sent_all(seconds, second_send)


def on_device(grid_count, pt_count, orbitals, point_index, factor_panels):
    own_bands, grid_rows = orbitals.shape
    rows_here = grid_rows // grid_count
    panel = point_index.shape[0]
    chunks = rows_here // LANES
    pairs = grid_count // 2
    pieces = rows_here // PIECE
    hbm = pl.BlockSpec(memory_space=pl.ANY)
    dma = pltpu.SemaphoreType.DMA
    square = [pltpu.VMEM((panel, panel), t) for t in (F32, F32, BF16, BF16, BF16, BF16)]
    scratch = [
        pltpu.VMEM((1, panel), I32),
        pltpu.VMEM((own_bands, grid_rows), BF16),
        pltpu.VMEM(factor_panels.shape, F32),
        pltpu.VMEM((chunks, own_bands, pairs * LANES), BF16),
        pltpu.VMEM((2, own_bands, panel), BF16),
        pltpu.VMEM((own_bands, panel), F32),
        pltpu.VMEM((grid_count, 8, LANES), F32),
        pltpu.VMEM((pairs, 8, panel), F32),
        pltpu.VMEM((pieces, pairs - 1, PIECE, panel), I16),
        pltpu.VMEM((pieces, pairs - 1, PIECE, panel), I16),
        *square,
        pltpu.VMEM((pieces, PIECE, panel), BF16),
        pltpu.VMEM((pieces, PIECE, panel), BF16),
    ]
    used = sum(s.dtype.itemsize * functools.reduce(lambda a, b: a * b, s.shape) for s in scratch)
    sems = [
        dma((grid_rows // min(1024, grid_rows),)),
        dma, dma,
        dma, dma((chunks,)),
        dma, dma,
        dma, dma((grid_count,)),
        *[dma, dma((pieces,))] * 3,
    ]
    args = [point_index.reshape(1, panel), orbitals, factor_panels]
    return pl.pallas_call(
        functools.partial(kernel, grid_count, pt_count),
        out_shape=jax.ShapeDtypeStruct((rows_here, panel), F32),
        in_specs=[hbm] * 3,
        out_specs=pl.BlockSpec(memory_space=pltpu.VMEM),
        scratch_shapes=scratch + sems,
        compiler_params=pltpu.CompilerParams(
            collective_id=0, has_side_effects=True, vmem_limit_bytes=used + 8 * 1024 * 1024
        ),
    )(*[pltpu.with_memory_space_constraint(a, pltpu.HBM) for a in args])


def solution(mesh):
    in_specs = (P("grid", None), P("pt"), P("pt", None))
    out_specs = P("grid", "pt")
    body = functools.partial(on_device, mesh.shape["grid"], mesh.shape["pt"])
    return jax.shard_map(
        body, mesh=mesh, in_specs=in_specs, out_specs=out_specs, check_vma=False
    )
```

```python
import contextlib
import functools
import jax
import jax.numpy as jnp
from jax import lax
from jax.experimental import pallas as pl
from jax.experimental.pallas import tpu as pltpu
from jax.sharding import PartitionSpec as P

MESH = pl.DeviceIdType.MESH
F32, BF16, I16, I32 = jnp.float32, jnp.bfloat16, jnp.int16, jnp.int32
LANES = 128
PIECE = 32
SMALL = 16
BLOCK = 256
HELPER = 3
TOP = 32000.0


def scope(_):
    return contextlib.nullcontext()


def split(value):
    high = value.astype(BF16)
    return high, (value - high.astype(F32)).astype(BF16)


def dot(a, b):
    return jnp.dot(a, b, preferred_element_type=F32)


def fine_dot(a, b):
    size = b.shape[1]
    a_high, a_low = split(a)
    b_high, b_low = split(b)
    if size > LANES:
        return dot(a_high, b_high) + (dot(a_high, b_low) + dot(a_low, b_high))
    left = jnp.concatenate([a_high, a_low], axis=1)
    top = jnp.concatenate([b_high, b_low], axis=1)
    bottom = jnp.concatenate([b_high, jnp.zeros_like(b_high)], axis=1)
    both = dot(left, jnp.concatenate([top, bottom], axis=0))
    return both[:, :size] + both[:, size:]


def over_bands(a, b):
    return lax.dot_general(a, b, (((0,), (0,)), ((), ())), preferred_element_type=F32)


def each(low, high, body):
    if high - low <= 4:
        for i in range(low, high):
            body(i)
    else:
        pl.loop(low, high)(body)


def invert_lower(low, inv):
    size = low.shape[0]
    blocks = size // LANES
    row = lax.broadcasted_iota(jnp.int32, (LANES, LANES), 0)
    col = lax.broadcasted_iota(jnp.int32, (LANES, LANES), 1)
    tiles, parts = [], []
    for i in range(blocks):
        at = slice(i * LANES, (i + 1) * LANES)
        tile = low[at, at]
        tiles.append(tile)
        part = jnp.where(row == col, 1.0 / jnp.where(row == col, tile, 1.0), 0.0)
        below = jnp.where((row >> 1 == col >> 1) & (row > col), tile, 0.0)
        down, across = jnp.sum(part, axis=1, keepdims=True), jnp.sum(part, axis=0, keepdims=True)
        parts.append(part - below * down * across)
    half = 2
    level = 1
    while half < LANES:
        rb, cb = row >> level, col >> level
        mask = ((rb >> 1) == (cb >> 1)) & (rb > cb)
        mids = [fine_dot(jnp.where(mask, tiles[i], 0.0), parts[i]) for i in range(blocks)]
        parts = [parts[i] - fine_dot(parts[i], mids[i]) for i in range(blocks)]
        half *= 2
        level += 1
    inv[...] = jnp.zeros_like(inv)
    for i in range(blocks):
        at = slice(i * LANES, (i + 1) * LANES)
        inv[at, at] = parts[i]
    width = LANES
    while width < size:
        for start in range(0, size, 2 * width):
            top = slice(start, start + width)
            bottom = slice(start + width, start + 2 * width)
            mid = fine_dot(low[bottom, top], inv[top, top])
            inv[bottom, top] = -fine_dot(inv[bottom, bottom], mid)
        width *= 2


def kernel(
    grid_count, pt_count, index, orb, fac, out,
    index_v, orb_v, fac_v, near, points, gathered, ramp, early, norms, scales, sent, came,
    low, inv, a_high, a_low, b_high, b_low, firsts, seconds,
    lead_index, lead_points, lead_sent, lead_came, lead_sums, c_high, c_low,
    load_sem, index_sem, fac_sem, near_send, near_recv, point_send, point_recv, norm_send, norm_recv,
    part_send, part_recv, first_send, first_recv, second_send, second_recv,
    give_send, index_recv, low_recv, swap_send, swap_recv, lead_point_send, lead_point_recv,
    lead_part_send, lead_part_recv, sum_send, sum_recv,
):
    me = lax.axis_index("grid")
    rank = lax.axis_index("pt")
    own_bands, grid_rows = orb.shape
    chunks = near.shape[0]
    panel = index.shape[1]
    pieces = LANES // PIECE
    rows_here = chunks * LANES
    core = lax.rem(me, 2)
    chip = lax.div(me, 2)
    partner = me + 1 - 2 * core
    pairs = grid_count // 2
    last = pt_count - 1
    depth = min(1024, grid_rows)
    steps = grid_rows // depth
    blocks = depth // BLOCK
    smalls = PIECE // SMALL
    wide = rows_here // PIECE
    helped = rows_here - LANES
    is_helper = rank == HELPER

    def load(s):
        at = pl.ds(pl.multiple_of(s * depth, depth), depth)
        return pltpu.make_async_copy(orb.at[:, at], orb_v.at[:, at], load_sem.at[s])

    load_index = pltpu.make_async_copy(index, index_v, index_sem)
    load_fac = pltpu.make_async_copy(fac, fac_v, fac_sem)
    load_index.start()
    each(0, steps, lambda s: load(s).start())
    load_fac.start()

    barrier = pltpu.get_barrier_semaphore()

    def greet(g, r):
        pl.semaphore_signal(barrier, inc=1, device_id=(g, r), device_id_type=MESH)

    @pl.loop(1, grid_count)
    def _(k):
        greet(lax.rem(me + k, grid_count), rank)

    @pl.when(rank > 0)
    def _():
        greet(me, rank - 1)

    @pl.when(rank < last)
    def _():
        greet(me, rank + 1)

    @pl.when(rank < 2)
    def _():
        greet(me, HELPER)

    @pl.when(is_helper)
    def _():
        greet(me, 0)
        greet(me, 1)

    steps_of = lax.broadcasted_iota(I32, (BLOCK, panel), 0).astype(F32).astype(BF16)
    ramp[...] = steps_of.reshape(ramp.shape)

    with scope("t_load"):
        load_index.wait()
        load(0).wait()

    def gather(part, ids, s):
        hots = []
        for j in range(blocks):
            at = jnp.clip(ids[...] - (s * depth + j * BLOCK), -1, BLOCK).astype(F32)
            at = jnp.broadcast_to(at, (SMALL, panel)).astype(BF16)
            hot = jnp.where(ramp[...] == at[None], jnp.ones((), BF16), jnp.zeros((), BF16))
            hots.append(hot.reshape(BLOCK, panel))
        gathered[...] += dot(part, jnp.concatenate(hots, axis=0))

    def columns_of(s):
        return orb_v[:, pl.ds(pl.multiple_of(s * depth, depth), depth)]

    def gather_own(s):
        @pl.when(s > 0)
        def _():
            load(s).wait()

        part = columns_of(s)
        gather(part, index_v, s)
        value = part.astype(F32)
        size = jnp.max(jnp.sum(value * value, axis=0, keepdims=True), axis=1, keepdims=True)
        norms[me] = jnp.maximum(norms[me], size)

    with scope("t_gather"):
        gathered[...] = jnp.zeros_like(gathered)
        norms[me] = jnp.zeros(norms.shape[1:], F32)
        pl.loop(0, steps - 1)(gather_own)

    with scope("t_barrier"):
        near_ranks = (
            jnp.where(rank > 0, 1, 0) + jnp.where(rank < last, 1, 0)
            + jnp.where(rank < 2, 1, 0) + jnp.where(is_helper, 2, 0)
        )
        for count in range(1, 5):

            @pl.when(near_ranks == count)
            def _():
                pl.semaphore_wait(barrier, grid_count - 1 + count)

    def near_copy(q, c):
        start = (2 * c + 1 - core) * rows_here + q * LANES
        return pltpu.make_async_remote_copy(
            src_ref=orb.at[:, pl.ds(pl.multiple_of(start, LANES), LANES)],
            dst_ref=near.at[q, :, pl.ds(pl.multiple_of(c * LANES, LANES), LANES)],
            send_sem=near_send,
            recv_sem=near_recv.at[min(q, 1)],
            device_id=(partner, rank),
            device_id_type=MESH,
        )

    each(0, pairs, lambda c: near_copy(0, c).start())

    strips = panel // LANES

    def strip(ref, b):
        return ref.at[pl.ds(b * LANES, LANES), pl.ds(0, (b + 1) * LANES)]

    def for_half(half, body):
        @pl.when(core == half)
        def _():
            for b in range(strips // 2):
                if b % 2 == half:
                    body(b)
                    body(strips - 1 - b)

    half_rows = (strips // 4) * (strips + 1) * LANES * LANES // panel

    def copy_to(src, dst, send_sem, recv_sem, g, r):
        return pltpu.make_async_remote_copy(
            src_ref=src, dst_ref=dst, send_sem=send_sem, recv_sem=recv_sem,
            device_id=(g, r), device_id_type=MESH,
        )

    @pl.when(rank == 0)
    def _():
        copy_to(index_v, lead_index, give_send.at[0], index_recv, me, HELPER).start()
        for half in range(2):
            for_half(half, lambda b: copy_to(
                strip(fac, b), strip(low, b), give_send.at[1], low_recv, me, HELPER).start())

    with scope("t_gather2"):
        pl.loop(steps - 1, steps)(gather_own)
        points[core] = gathered[...].astype(BF16)

    def norm_copy(g, target, recv_sem):
        return copy_to(norms.at[g], norms.at[g], norm_send, recv_sem, target, rank)

    def point_copy(buf, slot, send_sem, recv_sem):
        return copy_to(buf.at[slot], buf.at[slot], send_sem, recv_sem, partner, rank)

    point_copy(points, core, point_send, point_recv).start()
    norm_copy(me, partner, norm_recv.at[0]).start()

    def bound(c):
        return norms[2 * c, 0:1, 0:1] + norms[2 * c + 1, 0:1, 0:1]

    def widen(value):
        return jnp.broadcast_to(jnp.maximum(value, 1e-30), scales.shape[1:])

    def peer(i):
        if pairs == 4:
            x, y = lax.rem(chip, 2), lax.div(chip, 2)
            return [chip, 3 - chip, chip + 2 - 4 * y, chip + 1 - 2 * x][i]
        return lax.rem(chip + i, pairs)

    def source(i):
        return peer(i) if pairs == 4 else lax.rem(chip + pairs - i, pairs)

    def rows_of(q):
        return pl.ds(pl.multiple_of(q * LANES, LANES), LANES)

    def rows_at(start, size):
        return pl.ds(pl.multiple_of(start, size), size)

    def own_sums(q, c, buf):
        start = (2 * c + core) * rows_here + q * LANES
        return over_bands(orb_v[:, pl.ds(pl.multiple_of(start, LANES), LANES)], buf[core])

    def near_sums(q, c, buf):
        part = near[q, :, pl.ds(pl.multiple_of(c * LANES, LANES), LANES)]
        return over_bands(part, buf[1 - core])

    def encode(value):
        return jnp.round(value * scales[0, 0:1, :]).astype(I32).astype(I16)

    def await_all(part, sem):
        pltpu.make_async_copy(part, part, sem).wait()

    ready = pairs <= early.shape[0]
    if ready:
        with scope("t_early"):
            for i in range(pairs):
                early[i] = own_sums(0, peer(i), points)

    for q in range(1, chunks):
        each(0, pairs, lambda c: near_copy(q, c).start())

    @pl.loop(1, grid_count)
    def _(k):
        other = lax.rem(me + k, grid_count)

        @pl.when(other != partner)
        def _():
            norm_copy(me, other, norm_recv.at[1]).start()

    with scope("t_partner"):
        norm_copy(partner, me, norm_recv.at[0]).wait_recv()
        scales[0] = TOP / widen(bound(chip))
        point_copy(points, 1 - core, point_send, point_recv).wait_recv()

    def part_copy(start, size, p, i):
        return copy_to(
            sent.at[i - 1, rows_at(start, size)], came.at[i - 1, rows_at(start, size)],
            part_send, part_recv.at[p], 2 * peer(i) + core, rank,
        )

    def send_rows(start, size, p):
        each(1, pairs, lambda i: part_copy(start, size, p, i).start())

    def send_parts(q, begun):
        def sums(i):
            c = peer(i)
            return (early[i] if begun else own_sums(q, c, points)) + near_sums(q, c, points)

        with scope("t_parts"):

            def for_other(i):
                sent[i - 1, rows_of(q)] = encode(sums(i))

            each(1, pairs, for_other)
            start, middle = q * LANES, q * pieces + smalls - 1
            if isinstance(q, int):
                for k in range(smalls):
                    send_rows(k * SMALL, SMALL, k)
            else:
                send_rows(start, PIECE, middle)
            for j in range(1, pieces - 1):
                send_rows(start + j * PIECE, PIECE, middle + j)
            at, p = start + (pieces - 1) * PIECE, middle + pieces - 1

            @pl.when(q < chunks - 1)
            def _():
                send_rows(at, PIECE, p)

            @pl.when(q == chunks - 1)
            def _():
                for k in range(smalls):
                    send_rows(at + k * SMALL, SMALL, p + k)

            out[rows_of(q), :] = sums(0)

    with scope("t_near"):
        await_all(near.at[0], near_recv.at[0])
    send_parts(0, ready)

    def lead_part_copy(i):
        return copy_to(
            lead_sent.at[i - 1], lead_came.at[i - 1], lead_part_send, lead_part_recv,
            2 * peer(i) + core, rank,
        )

    with scope("t_lead"):
        @pl.when(is_helper)
        def _():
            copy_to(index_v, lead_index, give_send.at[0], index_recv, me, rank).wait_recv()
            gathered[...] = jnp.zeros_like(gathered)

            @pl.loop(0, steps)
            def _(s):
                gather(columns_of(s), lead_index, s)

            lead_points[core] = gathered[...].astype(BF16)
            point_copy(lead_points, core, lead_point_send, lead_point_recv).start()

    with scope("t_near"):
        await_all(near.at[pl.ds(1, chunks - 1)], near_recv.at[1])

    with scope("t_lead"):
        @pl.when(is_helper)
        def _():
            point_copy(lead_points, 1 - core, lead_point_send, lead_point_recv).wait_recv()

            def lead_parts(i):
                c = peer(i)
                total = own_sums(chunks - 1, c, lead_points) + near_sums(chunks - 1, c, lead_points)
                lead_sent[i - 1] = encode(total)
                lead_part_copy(i).start()

            each(1, pairs, lead_parts)
            lead_sums[...] = own_sums(chunks - 1, chip, lead_points) + near_sums(chunks - 1, chip, lead_points)

    @pl.when(rank > 0)
    def _():
        @pl.loop(1, chunks)
        def _(q):
            send_parts(q, False)

    with scope("t_invert"):
        load_fac.wait()

        @pl.when(rank < 2)
        def _():
            start = pl.multiple_of(rank * panel, panel)
            low[...] = fac_v[:, pl.ds(start, panel)]

        @pl.when(is_helper)
        def _():
            half_low = low.at[pl.ds(0, half_rows)]
            await_all(half_low, low_recv)
            for half in range(2):
                for_half(half, lambda b: copy_to(
                    strip(low, b), strip(low, b), swap_send, swap_recv, partner, rank).start())
            await_all(half_low, swap_recv)

        @pl.when((rank < 2) | is_helper)
        def _():
            invert_lower(low, inv)

        @pl.when(rank > 0)
        def _():
            a_high[...], a_low[...] = split(fac_v[:, 0:panel].T)

        @pl.when(rank == 0)
        def _():
            a_high[...], a_low[...] = split(inv[...].T)

        @pl.when(rank > 1)
        def _():
            b_high[...], b_low[...] = split(fac_v[:, panel : 2 * panel].T)

        @pl.when(rank == 1)
        def _():
            b_high[...], b_low[...] = split(inv[...].T)

        @pl.when(is_helper)
        def _():
            c_high[...], c_low[...] = split(inv[...].T)

    def chain(buf, start, size, target, send_sem, recv_sem):
        part = buf.at[rows_at(start, size)]
        return copy_to(part, part, send_sem, recv_sem, me, target)

    half = panel // 2

    def solve(value, high, low_part):
        size = value.shape[0]
        value_high, value_low = split(value)
        both = jnp.concatenate([value_high, value_low], axis=0)

        def columns(k, at):
            total = dot(both[:, k], high[k, at])
            return total[:size] + (dot(value_high[:, k], low_part[k, at]) + total[size:])

        left = columns(slice(0, half), slice(0, half))
        right = columns(slice(0, panel), slice(half, panel))
        return jnp.concatenate([left, right], axis=1)

    def apply(value, high, low_part):
        return dot(value, high[...]) + dot(value, low_part[...])

    final = [(helped + j * PIECE, PIECE, helped // PIECE + smalls - 1 + j) for j in range(pieces - 1)]
    for k in range(smalls):
        final.append((rows_here - PIECE + k * SMALL, SMALL, wide + smalls - 2 + k))

    with scope("t_norms"):
        await_all(norms.at[pl.ds(0, grid_count - 2)], norm_recv.at[1])

        def source_scale(i):
            scales[i] = widen(bound(source(i))) * (1.0 / TOP)

        each(1, pairs, source_scale)

    with scope("t_lead2"):
        @pl.when(is_helper)
        def _():
            await_all(lead_came, lead_part_recv)

            def add(i):
                lead_sums[...] += lead_came[i - 1].astype(I32).astype(F32) * scales[i, 0:1, :]

            each(1, pairs, add)
            firsts[helped:rows_here, :] = solve(lead_sums[...] * lead_sums[...], c_high, c_low).astype(BF16)
            for target in (1, 2):
                for start, size, p in final:
                    chain(firsts, start, size, target, first_send, first_recv.at[p]).start()
            copy_to(lead_sums, lead_sums, sum_send, sum_recv, me, 0).start()

    def process(start, size, p, given):
        here = rows_at(start, size)

        def pass_on(buf, send_sem, recv_sem, lowest):
            @pl.when((rank >= lowest) & (rank < last))
            def _():
                chain(buf, start, size, rank + 1, send_sem, recv_sem.at[p]).start()

        def collect():
            await_all(came.at[:, here], part_recv.at[p])

            def add(i):
                out[here, :] += came[i - 1, here].astype(I32).astype(F32) * scales[i, 0:1, :]

            each(1, pairs, add)
            out[here, :] = out[here, :] * out[here, :]

        with scope("t_came"):
            if given:
                pl.when(rank > 0)(collect)
            else:
                collect()

        with scope("t_first"):
            @pl.when(rank == 0)
            def _():
                if given:
                    total = lead_sums[rows_at(start - helped, size), :]
                    out[here, :] = solve(total * total, a_high, a_low)
                else:
                    first = solve(out[here, :], a_high, a_low)
                    firsts[here] = first.astype(BF16)
                    out[here, :] = first

            def take():
                chain(firsts, start, size, rank, first_send, first_recv.at[p]).wait_recv()

            if given:
                pl.when((rank > 0) & (rank != HELPER))(take)
            else:
                pl.when(rank > 0)(take)
            pass_on(firsts, first_send, first_recv, HELPER if given else 0)

        with scope("t_second"):
            @pl.when(rank > 0)
            def _():
                out[here, :] -= apply(firsts[here], a_high, a_low)

            @pl.when(rank == 1)
            def _():
                second = solve(out[here, :], b_high, b_low)
                seconds[here] = second.astype(BF16)
                out[here, :] = second

            @pl.when(rank > 1)
            def _():
                chain(seconds, start, size, rank, second_send, second_recv.at[p]).wait_recv()

            pass_on(seconds, second_send, second_recv, 1)

        with scope("t_last"):
            @pl.when(rank > 1)
            def _():
                out[here, :] -= apply(seconds[here], b_high, b_low)

    @pl.loop(0, smalls)
    def _(k):
        process(k * SMALL, SMALL, k, False)

    @pl.loop(1, helped // PIECE)
    def _(p):
        q = lax.div(p, pieces) + 1

        @pl.when((lax.rem(p, pieces) == 1) & (rank == 0) & (q < chunks - 1))
        def _():
            send_parts(q, False)

        process(p * PIECE, PIECE, p + smalls - 1, False)

    @pl.when(rank == 0)
    def _():
        await_all(lead_sums, sum_recv)

    @pl.loop(helped // PIECE, wide - 1)
    def _(p):
        process(p * PIECE, PIECE, p + smalls - 1, True)

    @pl.loop(0, smalls)
    def _(k):
        process((wide - 1) * PIECE + k * SMALL, SMALL, wide + smalls - 2 + k, True)

    with scope("t_drain"):
        await_all(near, near_send)
        await_all(norms.at[pl.ds(0, grid_count - 1)], norm_send)
        point_copy(points, core, point_send, point_recv).wait_send()

        @pl.when(rank == 0)
        def _():
            await_all(sent.at[:, pl.ds(0, helped)], part_send)
            copy_to(index_v, lead_index, give_send.at[0], index_recv, me, HELPER).wait_send()
            await_all(low.at[pl.ds(0, half_rows)], give_send.at[1])

        @pl.when(rank > 0)
        def _():
            await_all(sent, part_send)

        @pl.when(is_helper)
        def _():
            await_all(low.at[pl.ds(0, half_rows)], swap_send)
            point_copy(lead_points, core, lead_point_send, lead_point_recv).wait_send()
            await_all(lead_sent, lead_part_send)
            await_all(lead_sums, sum_send)
            await_all(firsts.at[pl.ds(0, 2 * LANES)], first_send)

        @pl.when((rank < HELPER) | (is_helper & (rank < last)))
        def _():
            await_all(firsts.at[pl.ds(0, helped)], first_send)

        @pl.when(is_helper & (rank < last))
        def _():
            await_all(firsts.at[pl.ds(0, LANES)], first_send)

        @pl.when((rank > HELPER) & (rank < last))
        def _():
            await_all(firsts, first_send)

        @pl.when((rank > 0) & (rank < last))
        def _():
            await_all(seconds, second_send)


def on_device(grid_count, pt_count, orbitals, point_index, factor_panels):
    own_bands, grid_rows = orbitals.shape
    rows_here = grid_rows // grid_count
    panel = point_index.shape[0]
    chunks = rows_here // LANES
    pairs = grid_count // 2
    pieces = rows_here // PIECE + 2 * (PIECE // SMALL - 1)
    hbm = pl.BlockSpec(memory_space=pl.ANY)
    dma = pltpu.SemaphoreType.DMA
    square = [pltpu.VMEM((panel, panel), t) for t in (F32, F32, BF16, BF16, BF16, BF16)]
    scratch = [
        pltpu.VMEM((1, panel), I32),
        pltpu.VMEM((own_bands, grid_rows), BF16),
        pltpu.VMEM(factor_panels.shape, F32),
        pltpu.VMEM((chunks, own_bands, pairs * LANES), BF16),
        pltpu.VMEM((2, own_bands, panel), BF16),
        pltpu.VMEM((own_bands, panel), F32),
        pltpu.VMEM((BLOCK // SMALL, SMALL, panel), BF16),
        pltpu.VMEM((4, LANES, panel), F32),
        pltpu.VMEM((grid_count, 8, LANES), F32),
        pltpu.VMEM((pairs, 8, panel), F32),
        pltpu.VMEM((pairs - 1, rows_here, panel), I16),
        pltpu.VMEM((pairs - 1, rows_here, panel), I16),
        *square,
        pltpu.VMEM((rows_here, panel), BF16),
        pltpu.VMEM((rows_here, panel), BF16),
        pltpu.VMEM((1, panel), I32),
        pltpu.VMEM((2, own_bands, panel), BF16),
        pltpu.VMEM((pairs - 1, LANES, panel), I16),
        pltpu.VMEM((pairs - 1, LANES, panel), I16),
        pltpu.VMEM((LANES, panel), F32),
        pltpu.VMEM((panel, panel), BF16),
        pltpu.VMEM((panel, panel), BF16),
    ]
    used = sum(s.dtype.itemsize * functools.reduce(lambda a, b: a * b, s.shape) for s in scratch)
    sems = [
        dma((grid_rows // min(1024, grid_rows),)),
        dma, dma,
        dma, dma((2,)),
        dma, dma,
        dma, dma((2,)),
        *[dma, dma((pieces,))] * 3,
        dma((2,)), *[dma] * 10,
    ]
    args = [point_index.reshape(1, panel), orbitals, factor_panels]
    return pl.pallas_call(
        functools.partial(kernel, grid_count, pt_count),
        out_shape=jax.ShapeDtypeStruct((rows_here, panel), F32),
        in_specs=[hbm] * 3,
        out_specs=pl.BlockSpec(memory_space=pltpu.VMEM),
        scratch_shapes=scratch + sems,
        compiler_params=pltpu.CompilerParams(
            collective_id=0, has_side_effects=True, vmem_limit_bytes=min(used + 8 * 1024 * 1024, 64 * 1024 * 1024 - 1024 * 1024)
        ),
    )(*[pltpu.with_memory_space_constraint(a, pltpu.HBM) for a in args])


def solution(mesh):
    in_specs = (P("grid", None), P("pt"), P("pt", None))
    out_specs = P("grid", "pt")
    body = functools.partial(on_device, mesh.shape["grid"], mesh.shape["pt"])
    return jax.shard_map(
        body, mesh=mesh, in_specs=in_specs, out_specs=out_specs, check_vma=False
    )
```

```python
import contextlib
import functools
import jax
import jax.numpy as jnp
from jax import lax
from jax.experimental import pallas as pl
from jax.experimental.pallas import tpu as pltpu
from jax.sharding import PartitionSpec as P

MESH = pl.DeviceIdType.MESH
F32, BF16, I16, I32 = jnp.float32, jnp.bfloat16, jnp.int16, jnp.int32
LANES = 128
PIECE = 32
SMALL = 16
BLOCK = 256
HELPER = 3
TOP = 32000.0


def scope(_):
    return contextlib.nullcontext()


def split(value):
    high = value.astype(BF16)
    return high, (value - high.astype(F32)).astype(BF16)


def dot(a, b):
    return jnp.dot(a, b, preferred_element_type=F32)


def fine_dot(a, b):
    size = b.shape[1]
    a_high, a_low = split(a)
    b_high, b_low = split(b)
    if size > LANES:
        return dot(a_high, b_high) + (dot(a_high, b_low) + dot(a_low, b_high))
    left = jnp.concatenate([a_high, a_low], axis=1)
    top = jnp.concatenate([b_high, b_low], axis=1)
    bottom = jnp.concatenate([b_high, jnp.zeros_like(b_high)], axis=1)
    both = dot(left, jnp.concatenate([top, bottom], axis=0))
    return both[:, :size] + both[:, size:]


def over_bands(a, b):
    return lax.dot_general(a, b, (((0,), (0,)), ((), ())), preferred_element_type=F32)


def each(low, high, body):
    if high - low <= 4:
        for i in range(low, high):
            body(i)
    else:
        pl.loop(low, high)(body)


def invert_lower(low, inv):
    size = low.shape[0]
    blocks = size // LANES
    row = lax.broadcasted_iota(jnp.int32, (LANES, LANES), 0)
    col = lax.broadcasted_iota(jnp.int32, (LANES, LANES), 1)
    tiles, parts = [], []
    for i in range(blocks):
        at = slice(i * LANES, (i + 1) * LANES)
        tile = low[at, at]
        tiles.append(tile)
        part = jnp.where(row == col, 1.0 / jnp.where(row == col, tile, 1.0), 0.0)
        below = jnp.where((row >> 1 == col >> 1) & (row > col), tile, 0.0)
        down, across = jnp.sum(part, axis=1, keepdims=True), jnp.sum(part, axis=0, keepdims=True)
        parts.append(part - below * down * across)
    half = 2
    level = 1
    while half < LANES:
        rb, cb = row >> level, col >> level
        mask = ((rb >> 1) == (cb >> 1)) & (rb > cb)
        mids = [fine_dot(jnp.where(mask, tiles[i], 0.0), parts[i]) for i in range(blocks)]
        parts = [parts[i] - fine_dot(parts[i], mids[i]) for i in range(blocks)]
        half *= 2
        level += 1
    inv[...] = jnp.zeros_like(inv)
    for i in range(blocks):
        at = slice(i * LANES, (i + 1) * LANES)
        inv[at, at] = parts[i]
    width = LANES
    while width < size:
        for start in range(0, size, 2 * width):
            top = slice(start, start + width)
            bottom = slice(start + width, start + 2 * width)
            mid = fine_dot(low[bottom, top], inv[top, top])
            inv[bottom, top] = -fine_dot(inv[bottom, bottom], mid)
        width *= 2


def kernel(
    grid_count, pt_count, index, orb, fac, out,
    index_v, orb_v, fac_v, near, points, gathered, ramp, early, norms, scales, sent, came,
    low, inv, a_high, a_low, b_high, b_low, firsts, seconds,
    lead_index, lead_points, lead_sent, lead_came, lead_sums, lead_code, lead_scale, c_high, c_low, relay_sent, relay_came, cross,
    load_sem, index_sem, fac_sem, near_send, near_recv, point_send, point_recv, norm_send, norm_recv,
    part_send, part_recv, first_send, first_recv, second_send, second_recv,
    give_send, index_recv, low_recv, swap_send, swap_recv, lead_point_send, lead_point_recv,
    lead_part_send, lead_part_recv, sum_send, sum_recv, relay_send, relay_recv, cross_send,
):
    me = lax.axis_index("grid")
    rank = lax.axis_index("pt")
    own_bands, grid_rows = orb.shape
    chunks = near.shape[0]
    panel = index.shape[1]
    pieces = LANES // PIECE
    rows_here = chunks * LANES
    core = lax.rem(me, 2)
    chip = lax.div(me, 2)
    partner = me + 1 - 2 * core
    pairs = grid_count // 2
    last = pt_count - 1
    depth = min(1024, grid_rows)
    steps = grid_rows // depth
    blocks = depth // BLOCK
    smalls = PIECE // SMALL
    wide = rows_here // PIECE
    helped = rows_here - LANES
    is_helper = rank == HELPER
    half = panel // 2
    first_cross = chunks - 2
    crossing = pairs == 4 and chunks >= 4

    def load(s):
        at = pl.ds(pl.multiple_of(s * depth, depth), depth)
        return pltpu.make_async_copy(orb.at[:, at], orb_v.at[:, at], load_sem.at[s])

    load_index = pltpu.make_async_copy(index, index_v, index_sem)
    load_fac = pltpu.make_async_copy(fac, fac_v, fac_sem)
    load_index.start()
    each(0, steps, lambda s: load(s).start())
    load_fac.start()

    barrier = pltpu.get_barrier_semaphore()

    def greet(g, r):
        pl.semaphore_signal(barrier, inc=1, device_id=(g, r), device_id_type=MESH)

    @pl.loop(1, grid_count)
    def _(k):
        greet(lax.rem(me + k, grid_count), rank)

    @pl.when(rank > 0)
    def _():
        greet(me, rank - 1)

    @pl.when(rank < last)
    def _():
        greet(me, rank + 1)

    @pl.when(rank < 2)
    def _():
        greet(me, HELPER)

    @pl.when(is_helper)
    def _():
        greet(me, 0)
        greet(me, 1)

    @pl.when((rank == 0) | (rank == 2))
    def _():
        greet(me, 2 - rank)

    steps_of = lax.broadcasted_iota(I32, (BLOCK, panel), 0).astype(F32).astype(BF16)
    ramp[...] = steps_of.reshape(ramp.shape)

    with scope("t_load"):
        load_index.wait()
        load(0).wait()

    def gather(part, ids, s):
        hots = []
        for j in range(blocks):
            at = jnp.clip(ids[...] - (s * depth + j * BLOCK), -1, BLOCK).astype(F32)
            at = jnp.broadcast_to(at, (SMALL, panel)).astype(BF16)
            hot = jnp.where(ramp[...] == at[None], jnp.ones((), BF16), jnp.zeros((), BF16))
            hots.append(hot.reshape(BLOCK, panel))
        gathered[...] += dot(part, jnp.concatenate(hots, axis=0))

    def columns_of(s):
        return orb_v[:, pl.ds(pl.multiple_of(s * depth, depth), depth)]

    def gather_own(s):
        @pl.when(s > 0)
        def _():
            load(s).wait()

        part = columns_of(s)
        gather(part, index_v, s)
        value = part.astype(F32)
        size = jnp.max(jnp.sum(value * value, axis=0, keepdims=True), axis=1, keepdims=True)
        norms[me] = jnp.maximum(norms[me], size)

    with scope("t_gather"):
        gathered[...] = jnp.zeros_like(gathered)
        norms[me] = jnp.zeros(norms.shape[1:], F32)
        pl.loop(0, steps - 1)(gather_own)

    with scope("t_barrier"):
        near_ranks = (
            jnp.where(rank > 0, 1, 0) + jnp.where(rank < last, 1, 0)
            + jnp.where(rank < 2, 1, 0) + jnp.where(is_helper, 2, 0)
            + jnp.where((rank == 0) | (rank == 2), 1, 0)
        )
        for count in range(1, 5):

            @pl.when(near_ranks == count)
            def _():
                pl.semaphore_wait(barrier, grid_count - 1 + count)

    def near_copy(q, c):
        start = (2 * c + 1 - core) * rows_here + q * LANES
        return pltpu.make_async_remote_copy(
            src_ref=orb.at[:, pl.ds(pl.multiple_of(start, LANES), LANES)],
            dst_ref=near.at[q, :, pl.ds(pl.multiple_of(c * LANES, LANES), LANES)],
            send_sem=near_send,
            recv_sem=near_recv.at[min(q, 1)],
            device_id=(partner, rank),
            device_id_type=MESH,
        )

    each(0, pairs, lambda c: near_copy(0, c).start())

    strips = panel // LANES

    def strip(ref, b):
        return ref.at[pl.ds(b * LANES, LANES), pl.ds(0, (b + 1) * LANES)]

    def for_half(half, body):
        @pl.when(core == half)
        def _():
            for b in range(strips // 2):
                if b % 2 == half:
                    body(b)
                    body(strips - 1 - b)

    half_rows = (strips // 4) * (strips + 1) * LANES * LANES // panel

    def copy_to(src, dst, send_sem, recv_sem, g, r):
        return pltpu.make_async_remote_copy(
            src_ref=src, dst_ref=dst, send_sem=send_sem, recv_sem=recv_sem,
            device_id=(g, r), device_id_type=MESH,
        )

    @pl.when(rank == 0)
    def _():
        copy_to(index_v, lead_index, give_send.at[0], index_recv, me, HELPER).start()
        for half in range(2):
            for_half(half, lambda b: copy_to(
                strip(fac, b), strip(low, b), give_send.at[1], low_recv, me, HELPER).start())

    with scope("t_gather2"):
        pl.loop(steps - 1, steps)(gather_own)
        points[core] = gathered[...].astype(BF16)

    def norm_copy(g, target, recv_sem):
        return copy_to(norms.at[g], norms.at[g], norm_send, recv_sem, target, rank)

    def point_copy(buf, slot, send_sem, recv_sem):
        return copy_to(buf.at[slot], buf.at[slot], send_sem, recv_sem, partner, rank)

    point_copy(points, core, point_send, point_recv).start()
    norm_copy(me, partner, norm_recv.at[0]).start()

    def bound(c):
        return norms[2 * c, 0:1, 0:1] + norms[2 * c + 1, 0:1, 0:1]

    def widen(value):
        return jnp.broadcast_to(jnp.maximum(value, 1e-30), scales.shape[1:])

    def peer(i):
        if pairs == 4:
            x, y = lax.rem(chip, 2), lax.div(chip, 2)
            return [chip, 3 - chip, chip + 2 - 4 * y, chip + 1 - 2 * x][i]
        return lax.rem(chip + i, pairs)

    def source(i):
        return peer(i) if pairs == 4 else lax.rem(chip + pairs - i, pairs)

    def rows_of(q):
        return pl.ds(pl.multiple_of(q * LANES, LANES), LANES)

    def rows_at(start, size):
        return pl.ds(pl.multiple_of(start, size), size)

    def own_sums(q, c, buf):
        start = (2 * c + core) * rows_here + q * LANES
        return over_bands(orb_v[:, pl.ds(pl.multiple_of(start, LANES), LANES)], buf[core])

    def near_sums(q, c, buf):
        part = near[q, :, pl.ds(pl.multiple_of(c * LANES, LANES), LANES)]
        return over_bands(part, buf[1 - core])

    def encode(value):
        return jnp.round(value * scales[0, 0:1, :]).astype(I32).astype(I16)

    def await_all(part, sem):
        pltpu.make_async_copy(part, part, sem).wait()

    ready = pairs <= early.shape[0]
    if ready:
        with scope("t_early"):
            for i in range(pairs):
                early[i] = own_sums(0, peer(i), points)

    for q in range(1, chunks):
        each(0, pairs, lambda c: near_copy(q, c).start())

    @pl.loop(1, grid_count)
    def _(k):
        other = lax.rem(me + k, grid_count)

        @pl.when(other != partner)
        def _():
            norm_copy(me, other, norm_recv.at[1]).start()

    with scope("t_partner"):
        norm_copy(partner, me, norm_recv.at[0]).wait_recv()
        scales[0] = TOP / widen(bound(chip))
        point_copy(points, 1 - core, point_send, point_recv).wait_recv()

    def part_copy(start, size, p, i, send_sem=part_send):
        return copy_to(
            sent.at[i - 1, rows_at(start, size)], came.at[i - 1, rows_at(start, size)],
            send_sem, part_recv.at[p], 2 * peer(i) + core, rank,
        )

    def send_rows(start, size, p):
        each(1, pairs, lambda i: part_copy(start, size, p, i).start())

    def send_parts(q, begun):
        def sums(i):
            c = peer(i)
            return (early[i] if begun else own_sums(q, c, points)) + near_sums(q, c, points)

        with scope("t_parts"):

            def for_other(i):
                sent[i - 1, rows_of(q)] = encode(sums(i))

            each(1, pairs, for_other)
            start, middle = q * LANES, q * pieces + smalls - 1
            if isinstance(q, int):
                for k in range(smalls):
                    send_rows(k * SMALL, SMALL, k)
            else:
                send_rows(start, PIECE, middle)
            for j in range(1, pieces - 1):
                send_rows(start + j * PIECE, PIECE, middle + j)
            at, p = start + (pieces - 1) * PIECE, middle + pieces - 1

            @pl.when(q < chunks - 1)
            def _():
                send_rows(at, PIECE, p)

            @pl.when(q == chunks - 1)
            def _():
                for k in range(smalls):
                    send_rows(at + k * SMALL, SMALL, p + k)

            out[rows_of(q), :] = sums(0)

    with scope("t_near"):
        await_all(near.at[0], near_recv.at[0])
    send_parts(0, ready)

    def lead_part_copy(i):
        return copy_to(
            lead_sent.at[i - 1], lead_came.at[i - 1], lead_part_send, lead_part_recv,
            2 * peer(i) + core, rank,
        )

    with scope("t_lead"):
        @pl.when(is_helper)
        def _():
            copy_to(index_v, lead_index, give_send.at[0], index_recv, me, rank).wait_recv()
            gathered[...] = jnp.zeros_like(gathered)

            @pl.loop(0, steps)
            def _(s):
                gather(columns_of(s), lead_index, s)

            lead_points[core] = gathered[...].astype(BF16)
            point_copy(lead_points, core, lead_point_send, lead_point_recv).start()

    def await_near():
        await_all(near.at[pl.ds(1, chunks - 1)], near_recv.at[1])

    with scope("t_near"):
        pl.when(rank > 0)(await_near)

    with scope("t_lead"):
        @pl.when(is_helper)
        def _():
            point_copy(lead_points, 1 - core, lead_point_send, lead_point_recv).wait_recv()

            def lead_parts(i):
                c = peer(i)
                total = own_sums(chunks - 1, c, lead_points) + near_sums(chunks - 1, c, lead_points)
                lead_sent[i - 1] = encode(total)
                lead_part_copy(i).start()

            each(1, pairs, lead_parts)
            lead_sums[...] = own_sums(chunks - 1, chip, lead_points) + near_sums(chunks - 1, chip, lead_points)

    def relay_copy(t, side):
        return copy_to(
            relay_sent.at[t, side], relay_came.at[t, side], relay_send, relay_recv.at[t],
            2 * peer(3 - side) + core, rank,
        )

    def cross_parts(t):
        q = first_cross + t
        code = encode(own_sums(q, peer(1), points) + near_sums(q, peer(1), points))
        relay_sent[t, 0] = code[:, :half]
        relay_sent[t, 1] = code[:, half:]
        relay_copy(t, 0).start()
        relay_copy(t, 1).start()
        for i in range(2):
            early[2 * t + i] = own_sums(q, peer(2 + i), points) + near_sums(q, peer(2 + i), points)
        out[rows_of(q), :] = own_sums(q, chip, points) + near_sums(q, chip, points)

    @pl.when(rank > 0)
    def _():
        if crossing:
            cross_parts(0)

        @pl.loop(1, first_cross if crossing else chunks)
        def _(q):
            send_parts(q, False)

        if crossing:
            cross_parts(1)

    with scope("t_invert"):
        load_fac.wait()

        @pl.when(rank < 2)
        def _():
            start = pl.multiple_of(rank * panel, panel)
            low[...] = fac_v[:, pl.ds(start, panel)]

        @pl.when(is_helper)
        def _():
            half_low = low.at[pl.ds(0, half_rows)]
            await_all(half_low, low_recv)
            for half in range(2):
                for_half(half, lambda b: copy_to(
                    strip(low, b), strip(low, b), swap_send, swap_recv, partner, rank).start())
            await_all(half_low, swap_recv)

        @pl.when((rank < 2) | is_helper)
        def _():
            invert_lower(low, inv)

        @pl.when(rank > 0)
        def _():
            a_high[...], a_low[...] = split(fac_v[:, 0:panel].T)

        @pl.when(rank == 0)
        def _():
            a_high[...], a_low[...] = split(inv[...].T)

        @pl.when(rank > 1)
        def _():
            b_high[...], b_low[...] = split(fac_v[:, panel : 2 * panel].T)

        @pl.when(rank == 1)
        def _():
            b_high[...], b_low[...] = split(inv[...].T)

        @pl.when(is_helper)
        def _():
            c_high[...], c_low[...] = split(inv[...].T)

    def chain(buf, start, size, target, send_sem, recv_sem):
        part = buf.at[rows_at(start, size)]
        return copy_to(part, part, send_sem, recv_sem, me, target)

    def solve(value, high, low_part):
        size = value.shape[0]
        value_high, value_low = split(value)
        both = jnp.concatenate([value_high, value_low], axis=0)

        def columns(k, at):
            total = dot(both[:, k], high[k, at])
            return total[:size] + (dot(value_high[:, k], low_part[k, at]) + total[size:])

        left = columns(slice(0, half), slice(0, half))
        right = columns(slice(0, panel), slice(half, panel))
        return jnp.concatenate([left, right], axis=1)

    def apply(value, high, low_part):
        return dot(value, high[...]) + dot(value, low_part[...])

    final = [(helped + j * PIECE, PIECE, helped // PIECE + smalls - 1 + j) for j in range(pieces - 1)]
    for k in range(smalls):
        final.append((rows_here - PIECE + k * SMALL, SMALL, wide + smalls - 2 + k))

    pl.when(rank == 0)(await_near)

    with scope("t_norms"):
        await_all(norms.at[pl.ds(0, grid_count - 2)], norm_recv.at[1])

        def source_scale(i):
            scales[i] = widen(bound(source(i))) * (1.0 / TOP)

        each(1, pairs, source_scale)

        if crossing:
            away, up, over = bound(peer(1)), bound(peer(2)), bound(peer(3))
            here_only = scales[0]
            cross[0, :, :half] = (TOP / widen(bound(chip) + over))[:, :half]
            cross[0, :, half:] = here_only[:, half:]
            cross[1, :, :half] = here_only[:, :half]
            cross[1, :, half:] = (TOP / widen(bound(chip) + up))[:, half:]
            cross[2, :, :half] = (widen(up + away) * (1.0 / TOP))[:, :half]
            cross[2, :, half:] = scales[2][:, half:]
            cross[3, :, :half] = scales[3][:, :half]
            cross[3, :, half:] = (widen(over + away) * (1.0 / TOP))[:, half:]

        lead_scale[...] = jnp.broadcast_to(bound(chip), lead_scale.shape)

        def include(i):
            lead_scale[...] += jnp.broadcast_to(bound(source(i)), lead_scale.shape)

        each(1, pairs, include)
        lead_scale[...] = jnp.maximum(lead_scale[...], 1e-30)

    with scope("t_lead2"):
        @pl.when(is_helper)
        def _():
            await_all(lead_came, lead_part_recv)

            def add(i):
                lead_sums[...] += lead_came[i - 1].astype(I32).astype(F32) * scales[i, 0:1, :]

            each(1, pairs, add)
            firsts[helped:rows_here, :] = solve(lead_sums[...] * lead_sums[...], c_high, c_low).astype(BF16)
            for target in (1, 2):
                for start, size, p in final:
                    chain(firsts, start, size, target, first_send, first_recv.at[p]).start()
            lead_code[...] = jnp.round(lead_sums[...] * (TOP / lead_scale[0:1, :])).astype(I32).astype(I16)
            copy_to(lead_code, lead_code, sum_send, sum_recv, me, 0).start()

    def relay(t):
        q = first_cross + t
        await_all(relay_came.at[t], relay_recv.at[t])

        def add(side, columns):
            value = relay_came[t, side].astype(I32).astype(F32) * scales[3 - side, 0:1, columns]
            early[2 * t + side, :, columns] += value

        add(0, slice(0, half))
        add(1, slice(half, panel))
        for i in range(2):
            value = early[2 * t + i] * cross[i, 0:1, :]
            sent[1 + i, rows_of(q)] = jnp.round(value).astype(I32).astype(I16)
        parts = final if t == 1 else [
            (q * LANES + j * PIECE, PIECE, q * pieces + smalls - 1 + j) for j in range(pieces)
        ]
        for start, size, p in parts:
            for i in (2, 3):
                part_copy(start, size, p, i, cross_send).start()

    def lead_ahead():
        for start, size, p in final:

            @pl.when(rank != HELPER)
            def _():
                chain(firsts, start, size, rank, first_send, first_recv.at[p]).wait_recv()

            @pl.when((rank >= HELPER) & (rank < last))
            def _():
                chain(firsts, start, size, rank + 1, first_send, first_recv.at[p]).start()

        lead_sums[...] = apply(firsts[helped:rows_here, :], a_high, a_low)

    def process(start, size, p, given, crossed=False, straight=False):
        here = rows_at(start, size)

        def pass_on(buf, send_sem, recv_sem, skipped):
            @pl.when((rank < last) & jnp.logical_not(skipped))
            def _():
                chain(buf, start, size, rank + 1, send_sem, recv_sem.at[p]).start()

        def collect():
            await_all(came.at[:, here], part_recv.at[p])

            def add(i):
                out[here, :] += came[i - 1, here].astype(I32).astype(F32) * scales[i, 0:1, :]

            each(1, pairs, add)
            out[here, :] = out[here, :] * out[here, :]

        def collect_cross():
            await_all(came.at[pl.ds(1, 2), here], part_recv.at[p])
            for i in range(2):
                out[here, :] += came[1 + i, here].astype(I32).astype(F32) * cross[2 + i, 0:1, :]
            out[here, :] = out[here, :] * out[here, :]

        with scope("t_came"):
            if not crossed:
                collect()
            else:
                pl.when(rank > 0)(collect_cross if crossing else collect)
                if not given:
                    pl.when(rank == 0)(collect)

        with scope("t_first"):
            @pl.when(rank == 0)
            def _():
                if given:
                    total = lead_code[rows_at(start - helped, size), :].astype(I32).astype(F32)
                    total = total * (lead_scale[0:1, :] * (1.0 / TOP))
                    out[here, :] = solve(total * total, a_high, a_low)
                else:
                    first = solve(out[here, :], a_high, a_low)
                    firsts[here] = first.astype(BF16)
                    out[here, :] = first

            if not given:
                @pl.when(rank > 0)
                def _():
                    chain(firsts, start, size, rank, first_send, first_recv.at[p]).wait_recv()

                pass_on(firsts, first_send, first_recv, (rank == 1) & straight)

                @pl.when((rank == 0) & straight)
                def _():
                    chain(firsts, start, size, 2, first_send, first_recv.at[p]).start()

        with scope("t_second"):
            @pl.when(rank > 0)
            def _():
                if given:
                    out[here, :] -= lead_sums[rows_at(start - helped, size), :]
                else:
                    out[here, :] -= apply(firsts[here], a_high, a_low)

            @pl.when(rank == 1)
            def _():
                second = solve(out[here, :], b_high, b_low)
                seconds[here] = second.astype(BF16)
                out[here, :] = second

            @pl.when(rank > 1)
            def _():
                chain(seconds, start, size, rank, second_send, second_recv.at[p]).wait_recv()

            pass_on(seconds, second_send, second_recv, rank == 0)

        with scope("t_last"):
            @pl.when(rank > 1)
            def _():
                out[here, :] -= apply(seconds[here], b_high, b_low)

    @pl.loop(0, smalls)
    def _(k):
        process(k * SMALL, SMALL, k, False, False, True)

    begin = first_cross * pieces

    @pl.loop(1, begin)
    def _(p):
        q = lax.div(p, pieces) + 1

        @pl.when((lax.rem(p, pieces) == 1) & (rank == 0) & (q < chunks - 1))
        def _():
            send_parts(q, False)

        process(p * PIECE, PIECE, p + smalls - 1, False, False, p < 2)

        if crossing:
            for t, due in ((0, pieces), (1, 2 * pieces - 1)):

                @pl.when((rank > 0) & (p == due))
                def _():
                    relay(t)

    @pl.loop(begin, helped // PIECE)
    def _(p):
        @pl.when((p == helped // PIECE - 1) & (rank > 0))
        def _():
            lead_ahead()

        process(p * PIECE, PIECE, p + smalls - 1, False, True)

    @pl.when(rank == 0)
    def _():
        await_all(lead_code, sum_recv)

    @pl.loop(helped // PIECE, wide - 1)
    def _(p):
        process(p * PIECE, PIECE, p + smalls - 1, True, True)

    @pl.loop(0, smalls)
    def _(k):
        process((wide - 1) * PIECE + k * SMALL, SMALL, wide + smalls - 2 + k, True, True)

    with scope("t_drain"):
        await_all(near, near_send)
        await_all(norms.at[pl.ds(0, grid_count - 1)], norm_send)
        point_copy(points, core, point_send, point_recv).wait_send()

        @pl.when(rank == 0)
        def _():
            await_all(sent.at[:, pl.ds(0, helped)], part_send)
            copy_to(index_v, lead_index, give_send.at[0], index_recv, me, HELPER).wait_send()
            await_all(low.at[pl.ds(0, half_rows)], give_send.at[1])

        @pl.when(rank > 0)
        def _():
            if crossing:
                direct = first_cross * LANES
                await_all(sent.at[:, pl.ds(0, direct)], part_send)
                await_all(sent.at[pl.ds(1, 2), pl.ds(direct, rows_here - direct)], cross_send)
                await_all(relay_sent, relay_send)
            else:
                await_all(sent, part_send)

        @pl.when(is_helper)
        def _():
            await_all(low.at[pl.ds(0, half_rows)], swap_send)
            point_copy(lead_points, core, lead_point_send, lead_point_recv).wait_send()
            await_all(lead_sent, lead_part_send)
            await_all(lead_code, sum_send)
            await_all(firsts.at[pl.ds(0, 2 * LANES)], first_send)

        for at, count in ((0, helped + 2 * PIECE), (1, helped - 2 * PIECE), (2, helped)):

            @pl.when(rank == at)
            def _():
                await_all(firsts.at[pl.ds(0, count)], first_send)

        @pl.when(is_helper & (rank < last))
        def _():
            await_all(firsts.at[pl.ds(0, helped)], first_send)

        @pl.when(is_helper & (rank < last))
        def _():
            await_all(firsts.at[pl.ds(0, LANES)], first_send)

        @pl.when((rank > HELPER) & (rank < last))
        def _():
            await_all(firsts, first_send)

        @pl.when((rank > 0) & (rank < last))
        def _():
            await_all(seconds, second_send)


def on_device(grid_count, pt_count, orbitals, point_index, factor_panels):
    own_bands, grid_rows = orbitals.shape
    rows_here = grid_rows // grid_count
    panel = point_index.shape[0]
    chunks = rows_here // LANES
    pairs = grid_count // 2
    pieces = rows_here // PIECE + 2 * (PIECE // SMALL - 1)
    hbm = pl.BlockSpec(memory_space=pl.ANY)
    dma = pltpu.SemaphoreType.DMA
    square = [pltpu.VMEM((panel, panel), t) for t in (F32, F32, BF16, BF16, BF16, BF16)]
    scratch = [
        pltpu.VMEM((1, panel), I32),
        pltpu.VMEM((own_bands, grid_rows), BF16),
        pltpu.VMEM(factor_panels.shape, F32),
        pltpu.VMEM((chunks, own_bands, pairs * LANES), BF16),
        pltpu.VMEM((2, own_bands, panel), BF16),
        pltpu.VMEM((own_bands, panel), F32),
        pltpu.VMEM((BLOCK // SMALL, SMALL, panel), BF16),
        pltpu.VMEM((4, LANES, panel), F32),
        pltpu.VMEM((grid_count, 8, LANES), F32),
        pltpu.VMEM((pairs, 8, panel), F32),
        pltpu.VMEM((pairs - 1, rows_here, panel), I16),
        pltpu.VMEM((pairs - 1, rows_here, panel), I16),
        *square,
        pltpu.VMEM((rows_here, panel), BF16),
        pltpu.VMEM((rows_here, panel), BF16),
        pltpu.VMEM((1, panel), I32),
        pltpu.VMEM((2, own_bands, panel), BF16),
        pltpu.VMEM((pairs - 1, LANES, panel), I16),
        pltpu.VMEM((pairs - 1, LANES, panel), I16),
        pltpu.VMEM((LANES, panel), F32),
        pltpu.VMEM((LANES, panel), I16),
        pltpu.VMEM((8, panel), F32),
        pltpu.VMEM((panel, panel), BF16),
        pltpu.VMEM((panel, panel), BF16),
        pltpu.VMEM((2, 2, LANES, panel // 2), I16),
        pltpu.VMEM((2, 2, LANES, panel // 2), I16),
        pltpu.VMEM((4, 8, panel), F32),
    ]
    used = sum(s.dtype.itemsize * functools.reduce(lambda a, b: a * b, s.shape) for s in scratch)
    sems = [
        dma((grid_rows // min(1024, grid_rows),)),
        dma, dma,
        dma, dma((2,)),
        dma, dma,
        dma, dma((2,)),
        *[dma, dma((pieces,))] * 3,
        dma((2,)), *[dma] * 11,
        dma((2,)), dma,
    ]
    args = [point_index.reshape(1, panel), orbitals, factor_panels]
    return pl.pallas_call(
        functools.partial(kernel, grid_count, pt_count),
        out_shape=jax.ShapeDtypeStruct((rows_here, panel), F32),
        in_specs=[hbm] * 3,
        out_specs=pl.BlockSpec(memory_space=pltpu.VMEM),
        scratch_shapes=scratch + sems,
        compiler_params=pltpu.CompilerParams(
            collective_id=0, has_side_effects=True, vmem_limit_bytes=min(used + 8 * 1024 * 1024, 64 * 1024 * 1024 - 1024 * 1024)
        ),
    )(*[pltpu.with_memory_space_constraint(a, pltpu.HBM) for a in args])


def solution(mesh):
    in_specs = (P("grid", None), P("pt"), P("pt", None))
    out_specs = P("grid", "pt")
    body = functools.partial(on_device, mesh.shape["grid"], mesh.shape["pt"])
    return jax.shard_map(
        body, mesh=mesh, in_specs=in_specs, out_specs=out_specs, check_vma=False
    )
```

```python
import contextlib
import functools
import jax
import jax.numpy as jnp
from jax import lax
from jax.experimental import pallas as pl
from jax.experimental.pallas import tpu as pltpu
from jax.sharding import PartitionSpec as P

MESH = pl.DeviceIdType.MESH
F32, BF16, I16, I32 = jnp.float32, jnp.bfloat16, jnp.int16, jnp.int32
LANES = 128
PIECE = 32
SMALL = 16
BLOCK = 256
HELPER = 3
TOP = 32000.0


def scope(_):
    return contextlib.nullcontext()


def split(value):
    high = value.astype(BF16)
    return high, (value - high.astype(F32)).astype(BF16)


def dot(a, b):
    return jnp.dot(a, b, preferred_element_type=F32)


def fine_dot(a, b):
    size = b.shape[1]
    a_high, a_low = split(a)
    b_high, b_low = split(b)
    if size > LANES:
        return dot(a_high, b_high) + (dot(a_high, b_low) + dot(a_low, b_high))
    left = jnp.concatenate([a_high, a_low], axis=1)
    top = jnp.concatenate([b_high, b_low], axis=1)
    bottom = jnp.concatenate([b_high, jnp.zeros_like(b_high)], axis=1)
    both = dot(left, jnp.concatenate([top, bottom], axis=0))
    return both[:, :size] + both[:, size:]


def over_bands(a, b):
    return lax.dot_general(a, b, (((0,), (0,)), ((), ())), preferred_element_type=F32)


def each(low, high, body):
    if high - low <= 4:
        for i in range(low, high):
            body(i)
    else:
        pl.loop(low, high)(body)


def invert_lower(low, inv):
    size = low.shape[0]
    blocks = size // LANES
    row = lax.broadcasted_iota(jnp.int32, (LANES, LANES), 0)
    col = lax.broadcasted_iota(jnp.int32, (LANES, LANES), 1)
    tiles, parts = [], []
    for i in range(blocks):
        at = slice(i * LANES, (i + 1) * LANES)
        tile = low[at, at]
        tiles.append(tile)
        part = jnp.where(row == col, 1.0 / jnp.where(row == col, tile, 1.0), 0.0)
        below = jnp.where((row >> 1 == col >> 1) & (row > col), tile, 0.0)
        down, across = jnp.sum(part, axis=1, keepdims=True), jnp.sum(part, axis=0, keepdims=True)
        parts.append(part - below * down * across)
    half = 2
    level = 1
    while half < LANES:
        rb, cb = row >> level, col >> level
        mask = ((rb >> 1) == (cb >> 1)) & (rb > cb)
        mids = [fine_dot(jnp.where(mask, tiles[i], 0.0), parts[i]) for i in range(blocks)]
        parts = [parts[i] - fine_dot(parts[i], mids[i]) for i in range(blocks)]
        half *= 2
        level += 1
    inv[...] = jnp.zeros_like(inv)
    for i in range(blocks):
        at = slice(i * LANES, (i + 1) * LANES)
        inv[at, at] = parts[i]
    width = LANES
    while width < size:
        for start in range(0, size, 2 * width):
            top = slice(start, start + width)
            bottom = slice(start + width, start + 2 * width)
            mid = fine_dot(low[bottom, top], inv[top, top])
            inv[bottom, top] = -fine_dot(inv[bottom, bottom], mid)
        width *= 2


def kernel(
    grid_count, pt_count, index, orb, fac, out,
    index_v, orb_v, fac_v, near, points, gathered, ramp, early, norms, scales, sent, came,
    low, inv, a_high, a_low, b_high, b_low, firsts, seconds,
    lead_index, lead_points, lead_sent, lead_came, lead_sums, lead_code, lead_scale, c_high, c_low, relay_sent, relay_came, cross,
    load_sem, index_sem, fac_sem, near_send, near_recv, point_send, point_recv, norm_send, norm_recv,
    part_send, part_recv, first_send, first_recv, second_send, second_recv,
    give_send, index_recv, low_recv, swap_send, swap_recv, lead_point_send, lead_point_recv,
    lead_part_send, lead_part_recv, sum_send, sum_recv, relay_send, relay_recv, cross_send,
):
    me = lax.axis_index("grid")
    rank = lax.axis_index("pt")
    own_bands, grid_rows = orb.shape
    chunks = near.shape[0]
    panel = index.shape[1]
    pieces = LANES // PIECE
    rows_here = chunks * LANES
    core = lax.rem(me, 2)
    chip = lax.div(me, 2)
    partner = me + 1 - 2 * core
    pairs = grid_count // 2
    last = pt_count - 1
    depth = min(1024, grid_rows)
    steps = grid_rows // depth
    blocks = depth // BLOCK
    smalls = PIECE // SMALL
    wide = rows_here // PIECE
    helped = rows_here - LANES
    is_helper = rank == HELPER
    half = panel // 2
    first_cross = chunks - 2
    crossing = pairs == 4 and chunks >= 4

    def load(s):
        at = pl.ds(pl.multiple_of(s * depth, depth), depth)
        return pltpu.make_async_copy(orb.at[:, at], orb_v.at[:, at], load_sem.at[s])

    load_index = pltpu.make_async_copy(index, index_v, index_sem)
    load_fac = pltpu.make_async_copy(fac, fac_v, fac_sem)
    load_index.start()
    each(0, steps, lambda s: load(s).start())

    barrier = pltpu.get_barrier_semaphore()

    def greet(g, r):
        pl.semaphore_signal(barrier, inc=1, device_id=(g, r), device_id_type=MESH)

    @pl.loop(1, grid_count)
    def _(k):
        greet(lax.rem(me + k, grid_count), rank)

    @pl.when(rank > 0)
    def _():
        greet(me, rank - 1)

    @pl.when(rank < last)
    def _():
        greet(me, rank + 1)

    @pl.when(rank < 2)
    def _():
        greet(me, HELPER)

    @pl.when(is_helper)
    def _():
        greet(me, 0)
        greet(me, 1)

    @pl.when((rank == 0) | (rank == 2))
    def _():
        greet(me, 2 - rank)

    steps_of = lax.broadcasted_iota(I32, (BLOCK, panel), 0).astype(F32).astype(BF16)
    ramp[...] = steps_of.reshape(ramp.shape)

    with scope("t_load"):
        load_index.wait()
        load(0).wait()
        load_fac.start()

    def gather(part, ids, s):
        hots = []
        for j in range(blocks):
            at = jnp.clip(ids[...] - (s * depth + j * BLOCK), -1, BLOCK).astype(F32)
            at = jnp.broadcast_to(at, (SMALL, panel)).astype(BF16)
            hot = jnp.where(ramp[...] == at[None], jnp.ones((), BF16), jnp.zeros((), BF16))
            hots.append(hot.reshape(BLOCK, panel))
        gathered[...] += dot(part, jnp.concatenate(hots, axis=0))

    def columns_of(s):
        return orb_v[:, pl.ds(pl.multiple_of(s * depth, depth), depth)]

    def gather_own(s):
        @pl.when(s > 0)
        def _():
            load(s).wait()

        part = columns_of(s)
        gather(part, index_v, s)
        value = part.astype(F32)
        size = jnp.max(jnp.sum(value * value, axis=0, keepdims=True), axis=1, keepdims=True)
        norms[me] = jnp.maximum(norms[me], size)

    with scope("t_gather"):
        gathered[...] = jnp.zeros_like(gathered)
        norms[me] = jnp.zeros(norms.shape[1:], F32)
        pl.loop(0, steps - 1)(gather_own)

    with scope("t_barrier"):
        near_ranks = (
            jnp.where(rank > 0, 1, 0) + jnp.where(rank < last, 1, 0)
            + jnp.where(rank < 2, 1, 0) + jnp.where(is_helper, 2, 0)
            + jnp.where((rank == 0) | (rank == 2), 1, 0)
        )
        for count in range(1, 5):

            @pl.when(near_ranks == count)
            def _():
                pl.semaphore_wait(barrier, grid_count - 1 + count)

    def near_copy(q, c):
        start = (2 * c + 1 - core) * rows_here + q * LANES
        return pltpu.make_async_remote_copy(
            src_ref=orb.at[:, pl.ds(pl.multiple_of(start, LANES), LANES)],
            dst_ref=near.at[q, :, pl.ds(pl.multiple_of(c * LANES, LANES), LANES)],
            send_sem=near_send,
            recv_sem=near_recv.at[min(q, 1)],
            device_id=(partner, rank),
            device_id_type=MESH,
        )

    each(0, pairs, lambda c: near_copy(0, c).start())

    strips = panel // LANES

    def strip(ref, b):
        return ref.at[pl.ds(b * LANES, LANES), pl.ds(0, (b + 1) * LANES)]

    def for_half(half, body):
        @pl.when(core == half)
        def _():
            for b in range(strips // 2):
                if b % 2 == half:
                    body(b)
                    body(strips - 1 - b)

    half_rows = (strips // 4) * (strips + 1) * LANES * LANES // panel

    def copy_to(src, dst, send_sem, recv_sem, g, r):
        return pltpu.make_async_remote_copy(
            src_ref=src, dst_ref=dst, send_sem=send_sem, recv_sem=recv_sem,
            device_id=(g, r), device_id_type=MESH,
        )

    @pl.when(rank == 0)
    def _():
        copy_to(index_v, lead_index, give_send.at[0], index_recv, me, HELPER).start()
        for half in range(2):
            for_half(half, lambda b: copy_to(
                strip(fac, b), strip(low, b), give_send.at[1], low_recv, me, HELPER).start())

    with scope("t_gather2"):
        pl.loop(steps - 1, steps)(gather_own)
        points[core] = gathered[...].astype(BF16)

    def norm_copy(g, target, recv_sem):
        return copy_to(norms.at[g], norms.at[g], norm_send, recv_sem, target, rank)

    def point_copy(buf, slot, send_sem, recv_sem):
        return copy_to(buf.at[slot], buf.at[slot], send_sem, recv_sem, partner, rank)

    point_copy(points, core, point_send, point_recv).start()
    norm_copy(me, partner, norm_recv.at[0]).start()

    def bound(c):
        return norms[2 * c, 0:1, 0:1] + norms[2 * c + 1, 0:1, 0:1]

    def widen(value):
        return jnp.broadcast_to(jnp.maximum(value, 1e-30), scales.shape[1:])

    def peer(i):
        if pairs == 4:
            x, y = lax.rem(chip, 2), lax.div(chip, 2)
            return [chip, 3 - chip, chip + 2 - 4 * y, chip + 1 - 2 * x][i]
        return lax.rem(chip + i, pairs)

    def source(i):
        return peer(i) if pairs == 4 else lax.rem(chip + pairs - i, pairs)

    def rows_of(q):
        return pl.ds(pl.multiple_of(q * LANES, LANES), LANES)

    def rows_at(start, size):
        return pl.ds(pl.multiple_of(start, size), size)

    def own_sums(q, c, buf):
        start = (2 * c + core) * rows_here + q * LANES
        return over_bands(orb_v[:, pl.ds(pl.multiple_of(start, LANES), LANES)], buf[core])

    def near_sums(q, c, buf):
        part = near[q, :, pl.ds(pl.multiple_of(c * LANES, LANES), LANES)]
        return over_bands(part, buf[1 - core])

    def encode(value):
        return jnp.round(value * scales[0, 0:1, :]).astype(I32).astype(I16)

    def await_all(part, sem):
        pltpu.make_async_copy(part, part, sem).wait()

    ready = pairs <= early.shape[0]
    if ready:
        with scope("t_early"):
            for i in range(pairs):
                early[i] = own_sums(0, peer(i), points)

    for q in range(1, chunks):
        each(0, pairs, lambda c: near_copy(q, c).start())

    @pl.loop(1, grid_count)
    def _(k):
        other = lax.rem(me + k, grid_count)

        @pl.when(other != partner)
        def _():
            norm_copy(me, other, norm_recv.at[1]).start()

    with scope("t_partner"):
        norm_copy(partner, me, norm_recv.at[0]).wait_recv()
        scales[0] = TOP / widen(bound(chip))
        point_copy(points, 1 - core, point_send, point_recv).wait_recv()

    def part_copy(start, size, p, i, send_sem=part_send):
        return copy_to(
            sent.at[i - 1, rows_at(start, size)], came.at[i - 1, rows_at(start, size)],
            send_sem, part_recv.at[p], 2 * peer(i) + core, rank,
        )

    def send_rows(start, size, p):
        each(1, pairs, lambda i: part_copy(start, size, p, i).start())

    def send_parts(q, begun):
        def sums(i):
            c = peer(i)
            return (early[i] if begun else own_sums(q, c, points)) + near_sums(q, c, points)

        with scope("t_parts"):

            def for_other(i):
                sent[i - 1, rows_of(q)] = encode(sums(i))

            each(1, pairs, for_other)
            start, middle = q * LANES, q * pieces + smalls - 1
            if isinstance(q, int):
                for k in range(smalls):
                    send_rows(k * SMALL, SMALL, k)
            else:
                send_rows(start, PIECE, middle)
            for j in range(1, pieces - 1):
                send_rows(start + j * PIECE, PIECE, middle + j)
            at, p = start + (pieces - 1) * PIECE, middle + pieces - 1

            @pl.when(q < chunks - 1)
            def _():
                send_rows(at, PIECE, p)

            @pl.when(q == chunks - 1)
            def _():
                for k in range(smalls):
                    send_rows(at + k * SMALL, SMALL, p + k)

            out[rows_of(q), :] = sums(0)

    with scope("t_near"):
        await_all(near.at[0], near_recv.at[0])
    send_parts(0, ready)

    def lead_part_copy(i):
        return copy_to(
            lead_sent.at[i - 1], lead_came.at[i - 1], lead_part_send, lead_part_recv,
            2 * peer(i) + core, rank,
        )

    with scope("t_lead"):
        @pl.when(is_helper)
        def _():
            copy_to(index_v, lead_index, give_send.at[0], index_recv, me, rank).wait_recv()
            gathered[...] = jnp.zeros_like(gathered)

            @pl.loop(0, steps)
            def _(s):
                gather(columns_of(s), lead_index, s)

            lead_points[core] = gathered[...].astype(BF16)
            point_copy(lead_points, core, lead_point_send, lead_point_recv).start()

    def await_near():
        await_all(near.at[pl.ds(1, chunks - 1)], near_recv.at[1])

    with scope("t_near"):
        pl.when(rank > 0)(await_near)

    with scope("t_lead"):
        @pl.when(is_helper)
        def _():
            point_copy(lead_points, 1 - core, lead_point_send, lead_point_recv).wait_recv()

            def lead_parts(i):
                c = peer(i)
                total = own_sums(chunks - 1, c, lead_points) + near_sums(chunks - 1, c, lead_points)
                lead_sent[i - 1] = encode(total)
                lead_part_copy(i).start()

            each(1, pairs, lead_parts)
            lead_sums[...] = own_sums(chunks - 1, chip, lead_points) + near_sums(chunks - 1, chip, lead_points)

    def relay_copy(t, side):
        return copy_to(
            relay_sent.at[t, side], relay_came.at[t, side], relay_send, relay_recv.at[t],
            2 * peer(3 - side) + core, rank,
        )

    def cross_parts(t):
        q = first_cross + t
        code = encode(own_sums(q, peer(1), points) + near_sums(q, peer(1), points))
        relay_sent[t, 0] = code[:, :half]
        relay_sent[t, 1] = code[:, half:]
        relay_copy(t, 0).start()
        relay_copy(t, 1).start()
        for i in range(2):
            early[2 * t + i] = own_sums(q, peer(2 + i), points) + near_sums(q, peer(2 + i), points)
        out[rows_of(q), :] = own_sums(q, chip, points) + near_sums(q, chip, points)

    @pl.when(rank > 0)
    def _():
        if crossing:
            cross_parts(0)

        @pl.loop(1, first_cross if crossing else chunks)
        def _(q):
            send_parts(q, False)

        if crossing:
            cross_parts(1)

    with scope("t_invert"):
        load_fac.wait()

        @pl.when(rank < 2)
        def _():
            start = pl.multiple_of(rank * panel, panel)
            low[...] = fac_v[:, pl.ds(start, panel)]

        @pl.when(is_helper)
        def _():
            half_low = low.at[pl.ds(0, half_rows)]
            await_all(half_low, low_recv)
            for half in range(2):
                for_half(half, lambda b: copy_to(
                    strip(low, b), strip(low, b), swap_send, swap_recv, partner, rank).start())
            await_all(half_low, swap_recv)

        @pl.when((rank < 2) | is_helper)
        def _():
            invert_lower(low, inv)

        @pl.when(rank > 0)
        def _():
            a_high[...], a_low[...] = split(fac_v[:, 0:panel].T)

        @pl.when(rank == 0)
        def _():
            a_high[...], a_low[...] = split(inv[...].T)

        @pl.when(rank > 1)
        def _():
            b_high[...], b_low[...] = split(fac_v[:, panel : 2 * panel].T)

        @pl.when(rank == 1)
        def _():
            b_high[...], b_low[...] = split(inv[...].T)

        @pl.when(is_helper)
        def _():
            c_high[...], c_low[...] = split(inv[...].T)

    def chain(buf, start, size, target, send_sem, recv_sem):
        part = buf.at[rows_at(start, size)]
        return copy_to(part, part, send_sem, recv_sem, me, target)

    def solve(value, high, low_part):
        size = value.shape[0]
        value_high, value_low = split(value)
        both = jnp.concatenate([value_high, value_low], axis=0)

        def columns(k, at):
            total = dot(both[:, k], high[k, at])
            return total[:size] + (dot(value_high[:, k], low_part[k, at]) + total[size:])

        left = columns(slice(0, half), slice(0, half))
        right = columns(slice(0, panel), slice(half, panel))
        return jnp.concatenate([left, right], axis=1)

    def apply(value, high, low_part):
        return dot(value, high[...]) + dot(value, low_part[...])

    final = [(helped + j * PIECE, PIECE, helped // PIECE + smalls - 1 + j) for j in range(pieces - 1)]
    for k in range(smalls):
        final.append((rows_here - PIECE + k * SMALL, SMALL, wide + smalls - 2 + k))

    pl.when(rank == 0)(await_near)

    with scope("t_norms"):
        await_all(norms.at[pl.ds(0, grid_count - 2)], norm_recv.at[1])

        def source_scale(i):
            scales[i] = widen(bound(source(i))) * (1.0 / TOP)

        each(1, pairs, source_scale)

        if crossing:
            away, up, over = bound(peer(1)), bound(peer(2)), bound(peer(3))
            here_only = scales[0]
            cross[0, :, :half] = (TOP / widen(bound(chip) + over))[:, :half]
            cross[0, :, half:] = here_only[:, half:]
            cross[1, :, :half] = here_only[:, :half]
            cross[1, :, half:] = (TOP / widen(bound(chip) + up))[:, half:]
            cross[2, :, :half] = (widen(up + away) * (1.0 / TOP))[:, :half]
            cross[2, :, half:] = scales[2][:, half:]
            cross[3, :, :half] = scales[3][:, :half]
            cross[3, :, half:] = (widen(over + away) * (1.0 / TOP))[:, half:]

        lead_scale[...] = jnp.broadcast_to(bound(chip), lead_scale.shape)

        def include(i):
            lead_scale[...] += jnp.broadcast_to(bound(source(i)), lead_scale.shape)

        each(1, pairs, include)
        lead_scale[...] = jnp.maximum(lead_scale[...], 1e-30)

    with scope("t_lead2"):
        @pl.when(is_helper)
        def _():
            await_all(lead_came, lead_part_recv)

            def add(i):
                lead_sums[...] += lead_came[i - 1].astype(I32).astype(F32) * scales[i, 0:1, :]

            each(1, pairs, add)
            firsts[helped:rows_here, :] = solve(lead_sums[...] * lead_sums[...], c_high, c_low).astype(BF16)
            for target in (1, 2):
                for start, size, p in final:
                    chain(firsts, start, size, target, first_send, first_recv.at[p]).start()
            lead_code[...] = jnp.round(lead_sums[...] * (TOP / lead_scale[0:1, :])).astype(I32).astype(I16)
            copy_to(lead_code, lead_code, sum_send, sum_recv, me, 0).start()

    def relay(t):
        q = first_cross + t
        await_all(relay_came.at[t], relay_recv.at[t])

        def add(side, columns):
            value = relay_came[t, side].astype(I32).astype(F32) * scales[3 - side, 0:1, columns]
            early[2 * t + side, :, columns] += value

        add(0, slice(0, half))
        add(1, slice(half, panel))
        for i in range(2):
            value = early[2 * t + i] * cross[i, 0:1, :]
            sent[1 + i, rows_of(q)] = jnp.round(value).astype(I32).astype(I16)
        parts = final if t == 1 else [
            (q * LANES + j * PIECE, PIECE, q * pieces + smalls - 1 + j) for j in range(pieces)
        ]
        for start, size, p in parts:
            for i in (2, 3):
                part_copy(start, size, p, i, cross_send).start()

    def lead_ahead():
        for start, size, p in final:

            @pl.when(rank != HELPER)
            def _():
                chain(firsts, start, size, rank, first_send, first_recv.at[p]).wait_recv()

            @pl.when((rank >= HELPER) & (rank < last))
            def _():
                chain(firsts, start, size, rank + 1, first_send, first_recv.at[p]).start()

        lead_sums[...] = apply(firsts[helped:rows_here, :], a_high, a_low)

    def process(start, size, p, given, crossed=False, straight=False):
        here = rows_at(start, size)

        def pass_on(buf, send_sem, recv_sem, skipped):
            @pl.when((rank < last) & jnp.logical_not(skipped))
            def _():
                chain(buf, start, size, rank + 1, send_sem, recv_sem.at[p]).start()

        def collect():
            await_all(came.at[:, here], part_recv.at[p])

            def add(i):
                out[here, :] += came[i - 1, here].astype(I32).astype(F32) * scales[i, 0:1, :]

            each(1, pairs, add)
            out[here, :] = out[here, :] * out[here, :]

        def collect_cross():
            await_all(came.at[pl.ds(1, 2), here], part_recv.at[p])
            for i in range(2):
                out[here, :] += came[1 + i, here].astype(I32).astype(F32) * cross[2 + i, 0:1, :]
            out[here, :] = out[here, :] * out[here, :]

        with scope("t_came"):
            if not crossed:
                collect()
            else:
                pl.when(rank > 0)(collect_cross if crossing else collect)
                if not given:
                    pl.when(rank == 0)(collect)

        with scope("t_first"):
            @pl.when(rank == 0)
            def _():
                if given:
                    total = lead_code[rows_at(start - helped, size), :].astype(I32).astype(F32)
                    total = total * (lead_scale[0:1, :] * (1.0 / TOP))
                    out[here, :] = solve(total * total, a_high, a_low)
                else:
                    first = solve(out[here, :], a_high, a_low)
                    firsts[here] = first.astype(BF16)
                    out[here, :] = first

            if not given:
                @pl.when(rank > 0)
                def _():
                    chain(firsts, start, size, rank, first_send, first_recv.at[p]).wait_recv()

                pass_on(firsts, first_send, first_recv, (rank == 1) & straight)

                @pl.when((rank == 0) & straight)
                def _():
                    chain(firsts, start, size, 2, first_send, first_recv.at[p]).start()

        with scope("t_second"):
            @pl.when(rank > 0)
            def _():
                if given:
                    out[here, :] -= lead_sums[rows_at(start - helped, size), :]
                else:
                    out[here, :] -= apply(firsts[here], a_high, a_low)

            @pl.when(rank == 1)
            def _():
                second = solve(out[here, :], b_high, b_low)
                seconds[here] = second.astype(BF16)
                out[here, :] = second

            @pl.when(rank > 1)
            def _():
                chain(seconds, start, size, rank, second_send, second_recv.at[p]).wait_recv()

            pass_on(seconds, second_send, second_recv, rank == 0)

        with scope("t_last"):
            @pl.when(rank > 1)
            def _():
                out[here, :] -= apply(seconds[here], b_high, b_low)

    @pl.loop(0, smalls)
    def _(k):
        process(k * SMALL, SMALL, k, False, False, True)

    begin = first_cross * pieces

    @pl.loop(1, begin)
    def _(p):
        q = lax.div(p, pieces) + 1

        @pl.when((lax.rem(p, pieces) == 1) & (rank == 0) & (q < chunks - 1))
        def _():
            send_parts(q, False)

        process(p * PIECE, PIECE, p + smalls - 1, False, False, p < 4)

        if crossing:
            for t, due in ((0, pieces), (1, 2 * pieces - 1)):

                @pl.when((rank > 0) & (p == due))
                def _():
                    relay(t)

    @pl.loop(begin, helped // PIECE)
    def _(p):
        @pl.when((p == helped // PIECE - 1) & (rank > 0))
        def _():
            lead_ahead()

        process(p * PIECE, PIECE, p + smalls - 1, False, True)

    @pl.when(rank == 0)
    def _():
        await_all(lead_code, sum_recv)

    @pl.loop(helped // PIECE, wide - 1)
    def _(p):
        process(p * PIECE, PIECE, p + smalls - 1, True, True)

    @pl.loop(0, smalls)
    def _(k):
        process((wide - 1) * PIECE + k * SMALL, SMALL, wide + smalls - 2 + k, True, True)

    with scope("t_drain"):
        await_all(near, near_send)
        await_all(norms.at[pl.ds(0, grid_count - 1)], norm_send)
        point_copy(points, core, point_send, point_recv).wait_send()

        @pl.when(rank == 0)
        def _():
            await_all(sent.at[:, pl.ds(0, helped)], part_send)
            copy_to(index_v, lead_index, give_send.at[0], index_recv, me, HELPER).wait_send()
            await_all(low.at[pl.ds(0, half_rows)], give_send.at[1])

        @pl.when(rank > 0)
        def _():
            if crossing:
                direct = first_cross * LANES
                await_all(sent.at[:, pl.ds(0, direct)], part_send)
                await_all(sent.at[pl.ds(1, 2), pl.ds(direct, rows_here - direct)], cross_send)
                await_all(relay_sent, relay_send)
            else:
                await_all(sent, part_send)

        @pl.when(is_helper)
        def _():
            await_all(low.at[pl.ds(0, half_rows)], swap_send)
            point_copy(lead_points, core, lead_point_send, lead_point_recv).wait_send()
            await_all(lead_sent, lead_part_send)
            await_all(lead_code, sum_send)
            await_all(firsts.at[pl.ds(0, 2 * LANES)], first_send)

        for at, count in ((0, helped + min(4 * PIECE, rows_here - helped)), (1, helped - 4 * PIECE), (2, helped)):

            @pl.when(rank == at)
            def _():
                await_all(firsts.at[pl.ds(0, count)], first_send)

        @pl.when(is_helper & (rank < last))
        def _():
            await_all(firsts.at[pl.ds(0, helped)], first_send)

        @pl.when(is_helper & (rank < last))
        def _():
            await_all(firsts.at[pl.ds(0, LANES)], first_send)

        @pl.when((rank > HELPER) & (rank < last))
        def _():
            await_all(firsts, first_send)

        @pl.when((rank > 0) & (rank < last))
        def _():
            await_all(seconds, second_send)


def on_device(grid_count, pt_count, orbitals, point_index, factor_panels):
    own_bands, grid_rows = orbitals.shape
    rows_here = grid_rows // grid_count
    panel = point_index.shape[0]
    chunks = rows_here // LANES
    pairs = grid_count // 2
    pieces = rows_here // PIECE + 2 * (PIECE // SMALL - 1)
    hbm = pl.BlockSpec(memory_space=pl.ANY)
    dma = pltpu.SemaphoreType.DMA
    square = [pltpu.VMEM((panel, panel), t) for t in (F32, F32, BF16, BF16, BF16, BF16)]
    scratch = [
        pltpu.VMEM((1, panel), I32),
        pltpu.VMEM((own_bands, grid_rows), BF16),
        pltpu.VMEM(factor_panels.shape, F32),
        pltpu.VMEM((chunks, own_bands, pairs * LANES), BF16),
        pltpu.VMEM((2, own_bands, panel), BF16),
        pltpu.VMEM((own_bands, panel), F32),
        pltpu.VMEM((BLOCK // SMALL, SMALL, panel), BF16),
        pltpu.VMEM((4, LANES, panel), F32),
        pltpu.VMEM((grid_count, 8, LANES), F32),
        pltpu.VMEM((pairs, 8, panel), F32),
        pltpu.VMEM((pairs - 1, rows_here, panel), I16),
        pltpu.VMEM((pairs - 1, rows_here, panel), I16),
        *square,
        pltpu.VMEM((rows_here, panel), BF16),
        pltpu.VMEM((rows_here, panel), BF16),
        pltpu.VMEM((1, panel), I32),
        pltpu.VMEM((2, own_bands, panel), BF16),
        pltpu.VMEM((pairs - 1, LANES, panel), I16),
        pltpu.VMEM((pairs - 1, LANES, panel), I16),
        pltpu.VMEM((LANES, panel), F32),
        pltpu.VMEM((LANES, panel), I16),
        pltpu.VMEM((8, panel), F32),
        pltpu.VMEM((panel, panel), BF16),
        pltpu.VMEM((panel, panel), BF16),
        pltpu.VMEM((2, 2, LANES, panel // 2), I16),
        pltpu.VMEM((2, 2, LANES, panel // 2), I16),
        pltpu.VMEM((4, 8, panel), F32),
    ]
    used = sum(s.dtype.itemsize * functools.reduce(lambda a, b: a * b, s.shape) for s in scratch)
    sems = [
        dma((grid_rows // min(1024, grid_rows),)),
        dma, dma,
        dma, dma((2,)),
        dma, dma,
        dma, dma((2,)),
        *[dma, dma((pieces,))] * 3,
        dma((2,)), *[dma] * 11,
        dma((2,)), dma,
    ]
    args = [point_index.reshape(1, panel), orbitals, factor_panels]
    return pl.pallas_call(
        functools.partial(kernel, grid_count, pt_count),
        out_shape=jax.ShapeDtypeStruct((rows_here, panel), F32),
        in_specs=[hbm] * 3,
        out_specs=pl.BlockSpec(memory_space=pltpu.VMEM),
        scratch_shapes=scratch + sems,
        compiler_params=pltpu.CompilerParams(
            collective_id=0, has_side_effects=True,
            vmem_limit_bytes=min(used + 8 * 1024 * 1024, 64 * 1024 * 1024 - 1024 * 1024)
        ),
    )(*[pltpu.with_memory_space_constraint(a, pltpu.HBM) for a in args])


def solution(mesh):
    in_specs = (P("grid", None), P("pt"), P("pt", None))
    out_specs = P("grid", "pt")
    body = functools.partial(on_device, mesh.shape["grid"], mesh.shape["pt"])
    return jax.shard_map(
        body, mesh=mesh, in_specs=in_specs, out_specs=out_specs, check_vma=False
    )
```
